32 devices in a mesh: groups: 2 (over y), tile: 4 (over z), pos: 4 (over x, core).
Axes of the slice: x: 2, y: 2, z: 4, core: 2. Of those that a mesh axis runs over, the one named last changes fastest.
Arguments:
- object_field: bfloat16 [2, 2048, 4096], P(None, ('groups', 'tile')), parts along dimension 1, may hold values from -6 to 6
- probe: float32 [4, 2, 256, 256], P('groups'), parts along dimension 0, may hold values from -6 to 6
- amplitude: bfloat16 [64, 256, 256], P(('groups', 'tile', 'pos')), parts along dimension 0, may hold values from 0.5 to 6
- offsets: int32 [64, 2], P(('groups', 'tile', 'pos')), parts along dimension 0, may hold values from 0 to 3840, as said below
- strip_owner: int32 [8], P('groups'), parts along dimension 0, may hold values from 0 to 3, each once
- chirp: float32 [256], replicated, may hold values from -3.140625 to 3.140625
Outputs:
- obj_grad: float32 [2, 2048, 4096], P(None, ('groups', 'tile'), 'pos'), parts along dimension 1
- probe_grad: float32 [4, 2, 256, 256], P('groups', None, 'pos'), parts along dimension 0
The draws below stay inside these ranges and needn't reach their ends.
There are 2 independent parts, one for each index of `groups`. The reference program is written for one: setup_inputs(seed, part) draws one part's arguments, and reference() takes and returns one part's arrays. A program takes and returns all parts, laid end to end along the dimension named above; an argument that names none is the same for every part. Nothing has to cross between parts.
Inputs may be any that keep to these rules, and one draw needn't show every extreme that they name: Position j's window covers object rows offsets[j, 0] to offsets[j, 0] + 255 and columns offsets[j, 1] to offsets[j, 1] + 255, inside the object of 1024 x 4096 cells. The 2 positions of one device differ by at most 128 in their rows and by at most 128 in their columns, and both differences are reached on every device. `strip_owner`: A permutation.
All inputs are finite; a program needn't handle non-finite values.
Results may differ from the reference program's by a relative error of at most 0.0003.
Values may be sent and summed in bfloat16 or wider, within the bound.
No kernel may reach another device: no remote copies, remote signals or barrier semaphores. Data moves between devices by JAX's collectives and lax.ppermute only.
A program may use at most 128 MiB of HBM per device.

```python
import math
import jax
import jax.numpy as jnp
from jax import lax

WIN = 256
MODES = 2
POS_DEV = 2
SPREAD = 128
OBJ_ROWS = 1024
OBJ_COLS = 4096
POSITIONS = 32
N_TILE = 4


def extreme_slots(key, devices_all, per_device):
    scores = jax.random.randint(key, (devices_all, per_device), 0, 1 << 20) * per_device + jnp.arange(per_device, dtype=jnp.int32)[None, :]
    order = jnp.argsort(scores, axis=1)
    return (order[:, 0], order[:, 1])


def spread_offsets(key, devices_all, per_device):
    key_raw, key_slot = jax.random.split(key)
    raw_steps = jax.random.randint(key_raw, (devices_all, per_device), 0, SPREAD + 1)
    low_slot, high_slot = extreme_slots(key_slot, devices_all, per_device)
    slot_ids = jnp.arange(per_device, dtype=jnp.int32)[None, :]
    raw_steps = jnp.where(slot_ids == low_slot[:, None], 0, raw_steps)
    return jnp.where(slot_ids == high_slot[:, None], SPREAD, raw_steps)


def draw_offsets(key, part):
    devices_all = POSITIONS // POS_DEV
    subkeys = jax.random.split(jax.random.fold_in(key, 17), 6)
    row_base = jax.random.randint(subkeys[0], (devices_all,), 0, OBJ_ROWS - WIN - SPREAD + 1)
    col_base = jax.random.randint(subkeys[1], (devices_all,), 0, OBJ_COLS - WIN - SPREAD + 1)
    row_pick = jax.random.randint(subkeys[2], (), 0, devices_all)
    col_pick = jax.random.randint(subkeys[3], (), 0, devices_all)
    row_base = row_base.at[row_pick].set(0)
    row_base = row_base.at[(row_pick + 1) % devices_all].set(OBJ_ROWS - WIN - SPREAD)
    col_base = col_base.at[col_pick].set(OBJ_COLS - WIN - SPREAD)
    rows_all = row_base[:, None] + spread_offsets(subkeys[4], devices_all, POS_DEV)
    cols_all = col_base[:, None] + spread_offsets(subkeys[5], devices_all, POS_DEV)
    return jnp.stack([rows_all, cols_all], axis=-1).reshape(POSITIONS, 2).astype(jnp.int32)


def shard_levels(key, dims, pieces, smallest, top_value):
    gain = 1.0
    for dim, shards_of in pieces:
        steps = jax.random.uniform(jax.random.fold_in(jax.random.fold_in(key, 6), dim), (shards_of,), jnp.float32, smallest / len(pieces), top_value / len(pieces))
        gain = gain * jnp.repeat(jnp.exp(steps), dims[dim] // shards_of).reshape((-1,) + (1,) * (len(dims) - 1 - dim))
    return gain


def centred(key, dims, scale, bound, cuts=(), held_as=jnp.bfloat16):
    gain = shard_levels(key, dims, cuts, -0.22, 0.18) if cuts else 1.0
    result = jax.random.normal(key, dims, jnp.float32) * scale * gain
    return jnp.minimum(jnp.maximum(result, -bound), bound).astype(held_as)


def setup_inputs(seed: int = 0, part: int = 0) -> dict:
    splits = jax.random.split(jax.random.key(seed), 7)
    part_splits = jax.random.split(jax.random.fold_in(splits[6], part), 7)
    object_field = centred(part_splits[0], (2, OBJ_ROWS, OBJ_COLS), 1.0, 6.0, ((1, 4),))
    probe = centred(part_splits[1], (MODES, 2, WIN, WIN), 1.0, 6.0, (), jnp.float32)
    amplitude = jnp.clip(jnp.exp(math.log(6.0) - 2.4849066 * jax.random.uniform(part_splits[2], (POSITIONS, WIN, WIN), jnp.float32) ** shard_levels(part_splits[2], (POSITIONS, WIN, WIN), ((0, 16),), -0.2, 0.2)), 0.5, 6.0).astype(jnp.bfloat16)
    offsets = draw_offsets(jax.random.fold_in(jax.random.fold_in(splits[6], part), 71), part)
    strip_owner = jax.random.permutation(part_splits[4], N_TILE).astype(jnp.int32)
    chirp = jnp.clip(jax.random.uniform(splits[5], (WIN,), jnp.float32, -3.140625, 3.140625), -3.140625, 3.140625)
    return {"object_field": object_field, "probe": probe, "amplitude": amplitude, "offsets": offsets, "strip_owner": strip_owner, "chirp": chirp}


HIGHEST_PREC = lax.Precision.HIGHEST

def build_propagator(chirp):
    win_size = chirp.shape[0]
    freq_index = jnp.arange(win_size, dtype=jnp.int32)
    phase_grid = 2.0 * math.pi / win_size * (freq_index[:, None] * freq_index[None, :] % win_size).astype(jnp.float32)
    unit_norm = 1.0 / math.sqrt(win_size)
    fourier_re = jnp.cos(phase_grid) * unit_norm
    fourier_im = -jnp.sin(phase_grid) * unit_norm
    chirp_re = jnp.cos(chirp)[:, None]
    chirp_im = jnp.sin(chirp)[:, None]
    middle_re = chirp_re * fourier_re - chirp_im * fourier_im
    middle_im = chirp_re * fourier_im + chirp_im * fourier_re
    prop_re = jnp.dot(fourier_re, middle_re, precision=HIGHEST_PREC) + jnp.dot(fourier_im, middle_im, precision=HIGHEST_PREC)
    prop_im = jnp.dot(fourier_re, middle_im, precision=HIGHEST_PREC) - jnp.dot(fourier_im, middle_re, precision=HIGHEST_PREC)
    return (prop_re, prop_im)

def apply_both(left_re, left_im, part_re, part_im):
    first_re = jnp.einsum('ab,...bc->...ac', left_re, part_re, precision=HIGHEST_PREC) - jnp.einsum('ab,...bc->...ac', left_im, part_im, precision=HIGHEST_PREC)
    first_im = jnp.einsum('ab,...bc->...ac', left_re, part_im, precision=HIGHEST_PREC) + jnp.einsum('ab,...bc->...ac', left_im, part_re, precision=HIGHEST_PREC)
    out_re = jnp.einsum('...ab,cb->...ac', first_re, left_re, precision=HIGHEST_PREC) - jnp.einsum('...ab,cb->...ac', first_im, left_im, precision=HIGHEST_PREC)
    out_im = jnp.einsum('...ab,cb->...ac', first_re, left_im, precision=HIGHEST_PREC) + jnp.einsum('...ab,cb->...ac', first_im, left_re, precision=HIGHEST_PREC)
    return (out_re, out_im)

def position_terms(window, probe, amplitude, prop_re, prop_im, grad_scale):
    obj_re = window[:, None, 0]
    obj_im = window[:, None, 1]
    probe_re = probe[None, :, 0]
    probe_im = probe[None, :, 1]
    exit_re = probe_re * obj_re - probe_im * obj_im
    exit_im = probe_re * obj_im + probe_im * obj_re
    far_re, far_im = apply_both(prop_re, prop_im, exit_re, exit_im)
    intensity = lax.optimization_barrier(jnp.sum(far_re * far_re + far_im * far_im, axis=1, keepdims=True))
    factor = (1.0 - amplitude[:, None].astype(jnp.float32) / jnp.maximum(jnp.sqrt(intensity), 1.0)) * grad_scale
    back_re, back_im = apply_both(prop_re.T, -prop_im.T, far_re * factor, far_im * factor)
    obj_part_re = lax.optimization_barrier(jnp.sum(probe_re * back_re + probe_im * back_im, axis=1))
    obj_part_im = lax.optimization_barrier(jnp.sum(probe_re * back_im - probe_im * back_re, axis=1))
    probe_part_re = lax.optimization_barrier(jnp.sum(obj_re * back_re + obj_im * back_im, axis=0))
    probe_part_im = lax.optimization_barrier(jnp.sum(obj_re * back_im - obj_im * back_re, axis=0))
    return (jnp.stack([obj_part_re, obj_part_im], axis=1), jnp.stack([probe_part_re, probe_part_im], axis=1))

def reference(object_field, probe, amplitude, offsets, strip_owner, chirp):
    strip_rows = OBJ_ROWS // N_TILE
    blocks = object_field.astype(jnp.float32).reshape(2, N_TILE, strip_rows, OBJ_COLS)
    whole_obj = blocks[:, strip_owner].reshape(2, OBJ_ROWS, OBJ_COLS)
    prop_re, prop_im = build_propagator(chirp)
    grad_scale = 1.0 / math.sqrt(POSITIONS)

    def advance(state_now, position):
        obj_acc, probe_acc = state_now
        corner, amp_now = position
        anchor = jnp.zeros((), jnp.int32)
        window = lax.dynamic_slice(whole_obj, (anchor, corner[0], corner[1]), (2, WIN, WIN))
        obj_part, probe_part = position_terms(window[None], probe, amp_now[None], prop_re, prop_im, grad_scale)
        current = lax.dynamic_slice(obj_acc, (anchor, corner[0], corner[1]), (2, WIN, WIN))
        obj_acc = lax.dynamic_update_slice(obj_acc, current + obj_part[0], (anchor, corner[0], corner[1]))
        return ((obj_acc, probe_acc + probe_part), None)
    start_state = (jnp.zeros((2, OBJ_ROWS, OBJ_COLS), jnp.float32), jnp.zeros((MODES, 2, WIN, WIN), jnp.float32))
    (obj_acc, probe_acc), _ = lax.scan(advance, start_state, (offsets, amplitude))
    natural = obj_acc.reshape(2, N_TILE, strip_rows, OBJ_COLS)
    owned = jnp.zeros_like(natural).at[:, strip_owner].set(natural)
    return (owned.reshape(2, OBJ_ROWS, OBJ_COLS), probe_acc)
```

```python
import functools
import math

import jax
import jax.numpy as jnp
from jax import lax
from jax.experimental import pallas as pl
from jax.experimental.pallas import tpu as pltpu
from jax.sharding import PartitionSpec as P

HIGHEST_PREC = lax.Precision.HIGHEST


def build_propagator(chirp):
    win_size = chirp.shape[0]
    freq_index = jnp.arange(win_size, dtype=jnp.int32)
    phase_grid = (
        2.0
        * math.pi
        / win_size
        * (freq_index[:, None] * freq_index[None, :] % win_size).astype(jnp.float32)
    )
    unit_norm = 1.0 / math.sqrt(win_size)
    fourier_re = jnp.cos(phase_grid) * unit_norm
    fourier_im = -jnp.sin(phase_grid) * unit_norm
    chirp_re = jnp.cos(chirp)[:, None]
    chirp_im = jnp.sin(chirp)[:, None]
    middle_re = chirp_re * fourier_re - chirp_im * fourier_im
    middle_im = chirp_re * fourier_im + chirp_im * fourier_re
    prop_re = jnp.dot(fourier_re, middle_re, precision=HIGHEST_PREC) + jnp.dot(
        fourier_im, middle_im, precision=HIGHEST_PREC
    )
    prop_im = jnp.dot(fourier_re, middle_im, precision=HIGHEST_PREC) - jnp.dot(
        fourier_im, middle_re, precision=HIGHEST_PREC
    )
    return (prop_re, prop_im)


def apply_both(left_re, left_im, part_re, part_im):
    first_re = jnp.einsum("ab,...bc->...ac", left_re, part_re, precision=HIGHEST_PREC) - jnp.einsum(
        "ab,...bc->...ac", left_im, part_im, precision=HIGHEST_PREC
    )
    first_im = jnp.einsum("ab,...bc->...ac", left_re, part_im, precision=HIGHEST_PREC) + jnp.einsum(
        "ab,...bc->...ac", left_im, part_re, precision=HIGHEST_PREC
    )
    out_re = jnp.einsum("...ab,cb->...ac", first_re, left_re, precision=HIGHEST_PREC) - jnp.einsum(
        "...ab,cb->...ac", first_im, left_im, precision=HIGHEST_PREC
    )
    out_im = jnp.einsum("...ab,cb->...ac", first_re, left_im, precision=HIGHEST_PREC) + jnp.einsum(
        "...ab,cb->...ac", first_im, left_re, precision=HIGHEST_PREC
    )
    return (out_re, out_im)


def position_terms(window, probe, amplitude, prop_re, prop_im, grad_scale):
    obj_re = window[:, None, 0]
    obj_im = window[:, None, 1]
    probe_re = probe[None, :, 0]
    probe_im = probe[None, :, 1]
    exit_re = probe_re * obj_re - probe_im * obj_im
    exit_im = probe_re * obj_im + probe_im * obj_re
    far_re, far_im = apply_both(prop_re, prop_im, exit_re, exit_im)
    intensity = jnp.sum(far_re * far_re + far_im * far_im, axis=1, keepdims=True)
    factor = (
        1.0 - amplitude[:, None].astype(jnp.float32) / jnp.maximum(jnp.sqrt(intensity), 1.0)
    ) * grad_scale
    back_re, back_im = apply_both(prop_re.T, -prop_im.T, far_re * factor, far_im * factor)
    obj_part_re = jnp.sum(probe_re * back_re + probe_im * back_im, axis=1)
    obj_part_im = jnp.sum(probe_re * back_im - probe_im * back_re, axis=1)
    probe_part_re = jnp.sum(obj_re * back_re + obj_im * back_im, axis=0)
    probe_part_im = jnp.sum(obj_re * back_im - obj_im * back_re, axis=0)
    return (
        jnp.stack([obj_part_re, obj_part_im], axis=1),
        jnp.stack([probe_part_re, probe_part_im], axis=1),
    )


def owner_of(strips, strip_owner):
    table = jnp.arange(strip_owner.shape[0], dtype=jnp.int32)
    return jnp.sum(jnp.where(strips[..., None] == table, strip_owner, 0), axis=-1)


def place_columns(strip_grad, start_cols, pieces):
    span_width = pieces.shape[-1]
    column_ids = start_cols[:, None] + jnp.arange(span_width, dtype=jnp.int32)[None, :]
    return strip_grad.at[:, :, column_ids].add(pieces.transpose(1, 2, 0, 3))


def per_device_general(object_field, probe, amplitude, offsets, strip_owner, chirp):
    tile_count = lax.axis_size("tile")
    pos_groups = lax.axis_size("pos")
    pos_count = amplitude.shape[0]
    win_size = probe.shape[-1]
    strip_rows = object_field.shape[1]
    width_all = object_field.shape[2]
    last_strip = tile_count - 1
    grad_scale = 1.0 / math.sqrt(pos_count * tile_count * pos_groups)
    prop_re, prop_im = build_propagator(chirp)
    everyone = lax.all_gather(offsets, "tile", axis=0, tiled=True)
    row_off = offsets[:, 0]
    strip_grad = jnp.zeros((2, strip_rows, width_all), jnp.float32)
    reach_strips = (win_size - 1) // strip_rows + 2
    flat_cols = everyone[:, 1]

    def cut_piece(start_col):
        return lax.dynamic_slice_in_dim(object_field, start_col, win_size, 2)

    pieces = jax.vmap(cut_piece)(flat_cols).reshape(tile_count, pos_count, 2, strip_rows, win_size)
    arrived = lax.all_to_all(pieces, "tile", split_axis=0, concat_axis=0, tiled=True)
    strip_of = row_off // strip_rows
    inside = row_off - strip_of * strip_rows
    strips = jnp.minimum(
        strip_of[:, None] + jnp.arange(reach_strips, dtype=jnp.int32)[None, :], last_strip
    )
    owners = owner_of(strips, strip_owner)
    slot_ids = jnp.arange(pos_count, dtype=jnp.int32)[:, None]
    stacked = (
        arrived[owners, slot_ids]
        .transpose(0, 2, 1, 3, 4)
        .reshape(pos_count, 2, reach_strips * strip_rows, win_size)
    )

    def cut_rows(stack_one, row_at):
        return lax.dynamic_slice_in_dim(stack_one, row_at, win_size, 1)

    windows = jax.vmap(cut_rows)(stacked, inside)
    obj_part, probe_sum = position_terms(
        windows.astype(jnp.float32), probe, amplitude, prop_re, prop_im, grad_scale
    )

    def put_rows(base_one, piece_one, row_at):
        return lax.dynamic_update_slice_in_dim(base_one, piece_one, row_at, 1)

    padded = jnp.zeros((pos_count, 2, reach_strips * strip_rows, win_size), jnp.float32)
    padded = jax.vmap(put_rows)(padded, obj_part, inside)
    split_grad = padded.reshape(pos_count, 2, reach_strips, strip_rows, win_size).transpose(
        0, 2, 1, 3, 4
    )
    outgoing = (
        jnp.zeros((tile_count, pos_count, 2, strip_rows, win_size), jnp.float32)
        .at[owners, slot_ids]
        .add(split_grad)
    )
    returned = lax.all_to_all(outgoing, "tile", split_axis=0, concat_axis=0, tiled=True)
    flat_back = returned.reshape(tile_count * pos_count, 2, strip_rows, win_size)
    strip_grad = place_columns(strip_grad, flat_cols, flat_back)
    strip_part = lax.psum_scatter(strip_grad, "pos", scatter_dimension=2, tiled=True)
    probe_total = lax.psum(probe_sum, ("tile", "pos"))
    row_share = win_size // pos_groups
    probe_out = lax.dynamic_slice_in_dim(
        probe_total, lax.axis_index("pos") * row_share, row_share, 2
    )
    return (strip_part, probe_out)


def strip_held(owner_ref, me, count):
    held = jnp.int32(0)
    for s in range(count):
        held = held + jnp.where(owner_ref[s] == me, s, 0).astype(jnp.int32)
    return held


def geometry(y_a, x_a, y_b, x_b):
    first = y_a < y_b
    return (
        jnp.where(first, y_a, y_b),
        jnp.where(first, x_a, x_b),
        jnp.where(first, x_b, x_a),
        first,
    )


def lane_iota(shape):
    return lax.broadcasted_iota(jnp.int32, shape, 1)


def row_iota(shape):
    return lax.broadcasted_iota(jnp.int32, shape, 0)


def pack_kernel(tiles, win, width, me_ref, owner_ref, *refs):
    offs = refs[:tiles]
    obj_ref = refs[tiles]
    outs = refs[tiles + 1 : 2 * tiles + 1]
    buf, pack, params, in_sem, out_sem = refs[2 * tiles + 1 :]
    half = win // 2
    quarter = win // 4
    strip = strip_held(owner_ref, me_ref[0], tiles)

    def fetch(k):
        start = pl.multiple_of(params[k, 3], 128)
        return pltpu.make_async_copy(
            obj_ref.at[:, :, pl.ds(start, 2 * win)], buf.at[k], in_sem.at[k]
        )

    for k in range(tiles):
        y_up, x_up, x_low, _ = geometry(offs[k][0, 0], offs[k][0, 1], offs[k][1, 0], offs[k][1, 1])
        left = jnp.minimum(x_up, x_low)
        params[k, 0] = y_up
        params[k, 1] = (x_low > x_up).astype(jnp.int32)
        params[k, 3] = jnp.minimum((left // 128) * 128, width - 2 * win)
        params[k, 2] = left - params[k, 3]
        fetch(k).start()

    def one(k, carry):
        fetch(k).wait()
        y_up = params[k, 0]
        right = params[k, 1]
        rem = params[k, 2]
        turn = lax.rem(half - rem, half)
        keep = lane_iota((quarter, half)) < half - rem
        base = strip * win
        for part in range(2):
            for chunk in range(2):
                outer = []
                for level in range(2):
                    row0 = level * half + chunk * quarter
                    wide = buf[k, part, row0 : row0 + quarter, :].astype(jnp.float32)
                    spun = [
                        pltpu.roll(wide[:, half * b : half * (b + 1)], turn, 1) for b in range(4)
                    ]
                    cols = [jnp.where(keep, spun[b], spun[b + 1]) for b in range(3)]
                    rows = base + row0 + row_iota((quarter, half))
                    in_upper = (rows < y_up + win).astype(jnp.int32)
                    low_first = in_upper == right
                    pack[k, part, row0 : row0 + quarter, 0:half] = jnp.where(
                        low_first, cols[0], cols[1]
                    ).astype(pack.dtype)
                    pack[k, part, row0 : row0 + quarter, half:win] = jnp.where(
                        low_first, cols[1], cols[2]
                    ).astype(pack.dtype)
                    outer.append(jnp.where(right == 1, cols[2], cols[0]))
                high = base + half + chunk * quarter + row_iota((quarter, half))
                use_high = (high >= y_up + half) & (high < y_up + win)
                pack[k, part, win : win + quarter, half * chunk : half * (chunk + 1)] = jnp.where(
                    use_high, outer[1], outer[0]
                ).astype(pack.dtype)
        return carry

    for k in range(tiles):
        one(k, 0)
        pltpu.make_async_copy(pack.at[k], outs[k], out_sem.at[k]).start()
    for k in range(tiles):
        pltpu.make_async_copy(pack.at[k], outs[k], out_sem.at[k]).wait()


def halves(x):
    high = x.astype(jnp.bfloat16)
    return high, (x - high.astype(jnp.float32)).astype(jnp.bfloat16)


def dot(a, b):
    return lax.dot_general(a, b, (((1,), (0,)), ((), ())), preferred_element_type=jnp.float32)


def rows_from(ref, part, start, count):
    down = pl.multiple_of((start // 8) * 8, 8)
    rows = ref[part, pl.ds(down, count + 8), :]
    return pltpu.roll(rows, lax.rem(count + 8 - (start - down), count + 8), 0)[0:count]


def rows_to(ref, part, start, blocks):
    down = pl.multiple_of((start // 8) * 8, 8)
    rows = jnp.concatenate(blocks + [jnp.zeros((8, blocks[0].shape[1]), jnp.float32)], axis=0)
    ref[part, pl.ds(down, rows.shape[0]), :] = pltpu.roll(rows, start - down, 0)


def compute_kernel(tiles, pos_groups, win, modes, grad_scale, me_ref, owner_ref, off_ref, *refs):
    packs = refs[:tiles]
    probe, amp, prop_re, prop_im, prop_t_re, prop_t_im, spot_ref = refs[tiles : tiles + 7]
    grads = refs[tiles + 7 : 2 * tiles + 7]
    pieces = refs[2 * tiles + 7 : 2 * tiles + 7 + pos_groups]
    (
        held, cat, wins, far, factor, right_a, right_b, left_a, left_b, obj_acc, probe_acc, gcat, outer_acc, gpack,
        in_sem, out_sem, piece_sem,
    ) = refs[2 * tiles + 7 + pos_groups :]
    half = win // 2
    quarter = win // 4
    me = me_ref[0]
    fetches = [pltpu.make_async_copy(packs[k], held.at[k], in_sem.at[k]) for k in range(tiles)]
    for fetch in fetches:
        fetch.start()

    for way in range(2):
        if way == 0:
            r_re, r_im = prop_t_re[...], prop_t_im[...]
            l_re, l_im = prop_re[...], prop_im[...]
        else:
            r_re, r_im = prop_re[...], -prop_im[...]
            l_re, l_im = prop_t_re[...], -prop_t_im[...]
        (rr, rr_low), (ri, ri_low) = halves(r_re), halves(r_im)
        for row, (a, b) in enumerate([(rr, ri), (rr, ri), (-ri, rr), (-ri, rr)]):
            right_a[way, row * win : (row + 1) * win, 0:win] = a
            right_a[way, row * win : (row + 1) * win, win : 2 * win] = b
        for row, (a, b) in enumerate([(rr_low, ri_low), (-ri_low, rr_low)]):
            right_b[way, row * win : (row + 1) * win, 0:win] = a
            right_b[way, row * win : (row + 1) * win, win : 2 * win] = b
        (lr, lr_low), (li, li_low) = halves(l_re), halves(l_im)
        for col, (a, b) in enumerate([(lr, li), (lr, li), (-li, lr), (-li, lr)]):
            left_a[way, 0:win, col * win : (col + 1) * win] = a
            left_a[way, win : 2 * win, col * win : (col + 1) * win] = b
        for col, (a, b) in enumerate([(lr_low, li_low), (-li_low, lr_low)]):
            left_b[way, 0:win, col * win : (col + 1) * win] = a
            left_b[way, win : 2 * win, col * win : (col + 1) * win] = b

    y_up, x_up, x_low, first = geometry(off_ref[0, 0], off_ref[0, 1], off_ref[1, 0], off_ref[1, 1])
    right = x_low > x_up
    strip = y_up // win
    rem = y_up - strip * win
    low_rem = lax.rem(rem, half)
    mid_block = (y_up + half) // half

    def slot_of(s):
        return lax.rem(me - owner_ref[jnp.minimum(s, tiles - 1)] + tiles, tiles)

    for fetch in fetches:
        fetch.wait()
    slots = [slot_of(strip + d) for d in range(3)]
    for part in range(2):
        for d in range(3):
            cat[part, d * win : (d + 1) * win, :] = held[slots[d], part, 0:win, :].astype(jnp.float32)
        for d in range(2):
            slot = slot_of((mid_block + d) // 2)
            for chunk in range(2):
                outer_acc[part, d * half + chunk * quarter : d * half + (chunk + 1) * quarter, :] = held[
                    slot, part, win : win + quarter, half * chunk : half * (chunk + 1)
                ].astype(jnp.float32)
    for part in range(2):
        upper = rows_from(cat, part, rem, win)
        wins[0, part] = upper
        wins[1, part, half:win, :] = rows_from(cat, part, rem + win, half)
        outer = rows_from(outer_acc, part, low_rem, half)
        wins[1, part, 0:half, 0:half] = jnp.where(right, upper[half:win, half:win], outer)
        wins[1, part, 0:half, half:win] = jnp.where(right, outer, upper[half:win, 0:half])

    def both(way, re, im):
        (re_h, re_l), (im_h, im_l) = halves(re), halves(im)
        mid = dot(jnp.concatenate([re_h, re_l, im_h, im_l], axis=1), right_a[way]) + dot(
            jnp.concatenate([re_h, im_h], axis=1), right_b[way]
        )
        (re_h, re_l), (im_h, im_l) = halves(mid[:, 0:win]), halves(mid[:, win : 2 * win])
        return dot(left_a[way], jnp.concatenate([re_h, re_l, im_h, im_l], axis=0)) + dot(
            left_b[way], jnp.concatenate([re_h, im_h], axis=0)
        )

    def forward(n, carry):
        q = n // modes
        m = lax.rem(n, modes)
        p_re, p_im = probe[m, 0], probe[m, 1]
        w_re, w_im = wins[q, 0], wins[q, 1]
        far[n] = both(0, p_re * w_re - p_im * w_im, p_re * w_im + p_im * w_re)
        return carry

    lax.fori_loop(0, 2 * modes, forward, 0)
    for q in range(2):
        total = jnp.zeros((win, win), jnp.float32)
        for m in range(modes):
            f_re, f_im = far[q * modes + m, 0:win, :], far[q * modes + m, win : 2 * win, :]
            total = total + (f_re * f_re + f_im * f_im)
        frame = jnp.where(first, q, 1 - q)
        measured = amp[frame].astype(jnp.float32)
        factor[q] = (1.0 - measured / jnp.maximum(jnp.sqrt(total), 1.0)) * grad_scale
    obj_acc[...] = jnp.zeros_like(obj_acc)
    probe_acc[...] = jnp.zeros_like(probe_acc)

    def backward(n, carry):
        q = n // modes
        m = lax.rem(n, modes)
        scale = factor[q]
        back = both(1, far[n, 0:win, :] * scale, far[n, win : 2 * win, :] * scale)
        b_re, b_im = back[0:win, :], back[win : 2 * win, :]
        p_re, p_im = probe[m, 0], probe[m, 1]
        w_re, w_im = wins[q, 0], wins[q, 1]
        obj_acc[q, 0] = obj_acc[q, 0] + (p_re * b_re + p_im * b_im)
        obj_acc[q, 1] = obj_acc[q, 1] + (p_re * b_im - p_im * b_re)
        probe_acc[m, 0] = probe_acc[m, 0] + (w_re * b_re + w_im * b_im)
        probe_acc[m, 1] = probe_acc[m, 1] + (w_re * b_im - w_im * b_re)
        return carry

    lax.fori_loop(0, 2 * modes, backward, 0)
    share = win // pos_groups
    spot = spot_ref[0]
    piece_copies = []
    for j in range(pos_groups):
        start = pl.multiple_of(jnp.bitwise_xor(spot, j) * share, share)
        piece_copies.append(
            pltpu.make_async_copy(
                probe_acc.at[:, :, pl.ds(start, share), :], pieces[j], piece_sem.at[j]
            )
        )
        piece_copies[-1].start()

    gcat[...] = jnp.zeros_like(gcat)
    outer_acc[...] = jnp.zeros_like(outer_acc)
    for part in range(2):
        low_a = obj_acc[1, part, 0:half, 0:half]
        low_b = obj_acc[1, part, 0:half, half:win]
        zero = jnp.zeros_like(low_a)
        obj_acc[0, part, half:win, 0:half] += jnp.where(right, zero, low_b)
        obj_acc[0, part, half:win, half:win] += jnp.where(right, low_a, zero)
        rows_to(gcat, part, rem, [obj_acc[0, part], obj_acc[1, part, half:win, :]])
        rows_to(outer_acc, part, low_rem, [jnp.where(right, low_b, low_a)])
        outer = outer_acc[part, 0:half, :] + outer_acc[part, half:win, :]
        for d in range(3):
            gpack[d, part, 0:win, :] = gcat[part, d * win : (d + 1) * win, :]
            for chunk in range(2):
                gpack[d, part, win : win + quarter, half * chunk : half * (chunk + 1)] = outer[
                    chunk * quarter : (chunk + 1) * quarter, :
                ]
    grad_copies = []
    for k in range(tiles):
        there = strip_held(owner_ref, lax.rem(me + k, tiles), tiles)
        d = jnp.clip(there - strip, 0, 2)
        grad_copies.append(pltpu.make_async_copy(gpack.at[d], grads[k], out_sem.at[k]))
        grad_copies[-1].start()
    for copy in piece_copies + grad_copies:
        copy.wait()


def place_kernel(tiles, pos_groups, win, slab, me_ref, spot_ref, owner_ref, *refs):
    count = tiles * pos_groups
    offs = refs[:pos_groups]
    packs = refs[pos_groups : pos_groups + count]
    parts_in = refs[pos_groups + count : pos_groups + count + tiles]
    out_ref, probe_ref = refs[pos_groups + count + tiles : pos_groups + count + tiles + 2]
    held, acc, probe_acc, params, in_sem, out_sem, part_sem = refs[pos_groups + count + tiles + 2 :]
    half = win // 2
    quarter = win // 4
    me = me_ref[0]
    strip = strip_held(owner_ref, me, tiles)
    base = strip * win
    first_col = spot_ref[0] * slab
    margin = 2 * win
    span = 3 * half
    rows_each = probe_acc.shape[2] // tiles
    part_copies = []
    for k in range(tiles):
        turn = lax.rem(me + tiles - k, tiles)
        start = pl.multiple_of(turn * rows_each, rows_each)
        part_copies.append(
            pltpu.make_async_copy(
                parts_in[k], probe_acc.at[:, :, pl.ds(start, rows_each), :], part_sem.at[k]
            )
        )
        part_copies[-1].start()

    for n in range(count):
        j, k = n // tiles, n % tiles
        off = offs[j]
        y_up, x_up, x_low, _ = geometry(off[2 * k, 0], off[2 * k, 1], off[2 * k + 1, 0], off[2 * k + 1, 1])
        left = jnp.minimum(x_up, x_low)
        hit = (y_up < base + win) & (y_up + span > base) & (left < first_col + slab) & (left + span > first_col)
        params[n, 0] = hit.astype(jnp.int32)
        params[n, 1] = y_up
        params[n, 2] = (x_low > x_up).astype(jnp.int32)
        params[n, 3] = left - first_col + margin

        @pl.when(hit)
        def _():
            pltpu.make_async_copy(packs[n], held.at[n], in_sem.at[n]).start()

    def clear(i, carry):
        acc[:, pl.ds(pl.multiple_of(i * 8, 8), 8), :] = jnp.zeros((2, 8, acc.shape[2]), jnp.float32)
        return carry

    lax.fori_loop(0, win // 8, clear, 0)
    for copy in part_copies:
        copy.wait()
    probe_out = pltpu.make_async_copy(probe_acc, probe_ref, part_sem.at[tiles])
    probe_out.start()

    def one(n, carry):
        @pl.when(params[n, 0] == 1)
        def _():
            pltpu.make_async_copy(packs[0], held.at[n], in_sem.at[n]).wait()
            y_up = params[n, 1]
            right = params[n, 2]
            col = params[n, 3]
            start = pl.multiple_of((col // 128) * 128, 128)
            rem = col - start
            lanes = lane_iota((quarter, half))
            stay = lanes >= rem

            for part in range(2):
                for chunk in range(4):
                    row0 = chunk * quarter
                    rows = base + row0 + row_iota((quarter, half))
                    low_first = (rows < y_up + win).astype(jnp.int32) == right
                    in_outer = (rows >= y_up + half) & (rows < y_up + win)
                    m0 = held[n, part, row0 : row0 + quarter, 0:half]
                    m1 = held[n, part, row0 : row0 + quarter, half:win]
                    side = held[n, part, win : win + quarter, half * (chunk % 2) : half * (chunk % 2 + 1)]
                    side = jnp.where(in_outer, side, 0.0)
                    cols = [
                        jnp.where(low_first, m0, jnp.where(right == 0, side, 0.0)),
                        jnp.where(low_first, m1, m0),
                        jnp.where(low_first, jnp.where(right == 1, side, 0.0), m1),
                    ]
                    spun = [pltpu.roll(c, rem, 1) for c in cols]
                    zero = jnp.zeros_like(m0)
                    shifted = [
                        jnp.where(stay, spun[0], zero),
                        jnp.where(stay, spun[1], spun[0]),
                        jnp.where(stay, spun[2], spun[1]),
                        jnp.where(stay, zero, spun[2]),
                    ]
                    for b in range(4):
                        at = pl.ds(pl.multiple_of(start + b * half, 128), half)
                        acc[part, row0 : row0 + quarter, at] += shifted[b]

        return carry

    lax.fori_loop(0, count, one, 0)
    out = pltpu.make_async_copy(acc.at[:, :, margin : margin + slab], out_ref, out_sem)
    out.start()
    out.wait()
    probe_out.wait()


def shifted(x, axis, count, k):
    return lax.ppermute(x, axis, [(i, (i + k) % count) for i in range(count)])


def swapped(x, axis, count, bit):
    return lax.ppermute(x, axis, [(i, i ^ bit) for i in range(count)])


def per_device_packed(object_field, probe, amplitude, offsets, strip_owner, chirp):
    tiles = lax.axis_size("tile")
    pos_groups = lax.axis_size("pos")
    pos_count, win, _ = amplitude.shape
    modes = probe.shape[0]
    width = object_field.shape[2]
    slab = width // pos_groups
    half = win // 2
    quarter = win // 4
    grad_scale = 1.0 / math.sqrt(pos_count * tiles * pos_groups)
    me = lax.axis_index("tile").astype(jnp.int32).reshape(1)
    spot = lax.axis_index("pos").astype(jnp.int32).reshape(1)
    smem = pl.BlockSpec(memory_space=pltpu.SMEM)
    vmem = pl.BlockSpec(memory_space=pltpu.VMEM)
    anywhere = pl.BlockSpec(memory_space=pl.ANY)
    pack_shape = (2, win + quarter, win)

    offs = [offsets] + [shifted(offsets, "tile", tiles, tiles - k) for k in range(1, tiles)]
    packs = pl.pallas_call(
        functools.partial(pack_kernel, tiles, win, width),
        out_shape=[jax.ShapeDtypeStruct(pack_shape, jnp.bfloat16)] * tiles,
        in_specs=[smem] * (2 + tiles) + [anywhere],
        out_specs=[anywhere] * tiles,
        scratch_shapes=[
            pltpu.VMEM((tiles, 2, win, 2 * win), jnp.bfloat16),
            pltpu.VMEM((tiles,) + pack_shape, jnp.bfloat16),
            pltpu.SMEM((tiles, 4), jnp.int32),
            pltpu.SemaphoreType.DMA((tiles,)),
            pltpu.SemaphoreType.DMA((tiles,)),
        ],
        name="pack",
    )(me, strip_owner, *offs, object_field)
    arrived = [packs[0]] + [shifted(packs[k], "tile", tiles, k) for k in range(1, tiles)]
    prop_re, prop_im = build_propagator(chirp)
    results = pl.pallas_call(
        functools.partial(compute_kernel, tiles, pos_groups, win, modes, grad_scale),
        out_shape=[jax.ShapeDtypeStruct(pack_shape, jnp.float32)] * tiles
        + [jax.ShapeDtypeStruct((modes, 2, win // pos_groups, win), jnp.float32)] * pos_groups,
        in_specs=[smem] * 3 + [anywhere] * tiles + [vmem] * 6 + [smem],
        out_specs=[anywhere] * (tiles + pos_groups),
        scratch_shapes=[
            pltpu.VMEM((tiles,) + pack_shape, jnp.bfloat16),
            pltpu.VMEM((2, 3 * win, win), jnp.float32),
            pltpu.VMEM((2, 2, win, win), jnp.float32),
            pltpu.VMEM((2 * modes, 2 * win, win), jnp.float32),
            pltpu.VMEM((2, win, win), jnp.float32),
            pltpu.VMEM((2, 4 * win, 2 * win), jnp.bfloat16),
            pltpu.VMEM((2, 2 * win, 2 * win), jnp.bfloat16),
            pltpu.VMEM((2, 2 * win, 4 * win), jnp.bfloat16),
            pltpu.VMEM((2, 2 * win, 2 * win), jnp.bfloat16),
            pltpu.VMEM((2, 2, win, win), jnp.float32),
            pltpu.VMEM((modes, 2, win, win), jnp.float32),
            pltpu.VMEM((2, 3 * win, win), jnp.float32),
            pltpu.VMEM((2, win, half), jnp.float32),
            pltpu.VMEM((3,) + pack_shape, jnp.float32),
            pltpu.SemaphoreType.DMA((tiles,)),
            pltpu.SemaphoreType.DMA((tiles,)),
            pltpu.SemaphoreType.DMA((pos_groups,)),
        ],
        name="propagate",
    )(me, strip_owner, offsets, *arrived, probe, amplitude, prop_re, prop_im, prop_re.T, prop_im.T, spot)
    grads, pieces = results[:tiles], list(results[tiles:])

    column = [grads[0]] + [shifted(grads[k], "tile", tiles, k) for k in range(1, tiles)]
    column_offs = [jnp.concatenate([offs[(tiles - k) % tiles] for k in range(tiles)], axis=0)]
    columns = [column]
    bit = pos_groups // 2
    while bit:
        columns = columns + [[swapped(x, "pos", pos_groups, bit) for x in c] for c in columns]
        column_offs = column_offs + [swapped(o, "pos", pos_groups, bit) for o in column_offs]
        bit //= 2

    bit = 1
    while len(pieces) > 1:
        pieces = [
            pieces[j] + swapped(pieces[j + 1], "pos", pos_groups, bit) for j in range(0, len(pieces), 2)
        ]
        bit *= 2
    mine = pieces[0]
    each = mine.shape[2] // tiles
    total = lax.dynamic_slice_in_dim(mine, me[0] * each, each, 2)
    for k in range(1, tiles):
        sent = lax.dynamic_slice_in_dim(mine, lax.rem(me[0] + k, tiles) * each, each, 2)
        total = total + shifted(sent, "tile", tiles, k)
    totals = [total] + [shifted(total, "tile", tiles, k) for k in range(1, tiles)]

    flat = [x for c in columns for x in c]
    count = len(flat)
    strip_part, probe_out = pl.pallas_call(
        functools.partial(place_kernel, tiles, pos_groups, win, slab),
        out_shape=[
            jax.ShapeDtypeStruct((2, win, slab), jnp.float32),
            jax.ShapeDtypeStruct((modes, 2, win // pos_groups, win), jnp.float32),
        ],
        in_specs=[smem] * (3 + pos_groups) + [anywhere] * (count + tiles),
        out_specs=[anywhere, anywhere],
        scratch_shapes=[
            pltpu.VMEM((count,) + pack_shape, jnp.float32),
            pltpu.VMEM((2, win, slab + 4 * win), jnp.float32),
            pltpu.VMEM((modes, 2, win // pos_groups, win), jnp.float32),
            pltpu.SMEM((count, 4), jnp.int32),
            pltpu.SemaphoreType.DMA((count,)),
            pltpu.SemaphoreType.DMA,
            pltpu.SemaphoreType.DMA((tiles + 1,)),
        ],
        name="place",
    )(me, spot, strip_owner, *column_offs, *flat, *totals)
    return (strip_part, probe_out)


def per_device(object_field, probe, amplitude, offsets, strip_owner, chirp):
    tiles = lax.axis_size("tile")
    pos_groups = lax.axis_size("pos")
    pos_count, win, _ = amplitude.shape
    width = object_field.shape[2]
    packed = (
        pos_count == 2
        and object_field.shape[1] == win
        and win == 256
        and pos_groups & (pos_groups - 1) == 0
        and width // pos_groups >= 2 * win
        and (width // pos_groups) % 128 == 0
        and (win // pos_groups) % (8 * tiles) == 0
    )
    plan = per_device_packed if packed else per_device_general
    return plan(object_field, probe, amplitude, offsets, strip_owner, chirp)


def solution(mesh):
    return jax.shard_map(
        per_device,
        mesh=mesh,
        in_specs=(
            P(None, ("groups", "tile"), None),
            P("groups", None, None, None),
            P(("groups", "tile", "pos"), None, None),
            P(("groups", "tile", "pos"), None),
            P("groups"),
            P(),
        ),
        out_specs=(P(None, ("groups", "tile"), "pos"), P("groups", None, "pos", None)),
        check_vma=False,
    )
```

```python
import functools
import math

import jax
import jax.numpy as jnp
from jax import lax
from jax.experimental import pallas as pl
from jax.experimental.pallas import tpu as pltpu
from jax.sharding import PartitionSpec as P

HIGHEST_PREC = lax.Precision.HIGHEST


def build_propagator(chirp):
    win_size = chirp.shape[0]
    freq_index = jnp.arange(win_size, dtype=jnp.int32)
    phase_grid = (
        2.0
        * math.pi
        / win_size
        * (freq_index[:, None] * freq_index[None, :] % win_size).astype(jnp.float32)
    )
    unit_norm = 1.0 / math.sqrt(win_size)
    fourier_re = jnp.cos(phase_grid) * unit_norm
    fourier_im = -jnp.sin(phase_grid) * unit_norm
    chirp_re = jnp.cos(chirp)[:, None]
    chirp_im = jnp.sin(chirp)[:, None]
    middle_re = chirp_re * fourier_re - chirp_im * fourier_im
    middle_im = chirp_re * fourier_im + chirp_im * fourier_re
    prop_re = jnp.dot(fourier_re, middle_re, precision=HIGHEST_PREC) + jnp.dot(
        fourier_im, middle_im, precision=HIGHEST_PREC
    )
    prop_im = jnp.dot(fourier_re, middle_im, precision=HIGHEST_PREC) - jnp.dot(
        fourier_im, middle_re, precision=HIGHEST_PREC
    )
    return (prop_re, prop_im)


def apply_both(left_re, left_im, part_re, part_im):
    first_re = jnp.einsum("ab,...bc->...ac", left_re, part_re, precision=HIGHEST_PREC) - jnp.einsum(
        "ab,...bc->...ac", left_im, part_im, precision=HIGHEST_PREC
    )
    first_im = jnp.einsum("ab,...bc->...ac", left_re, part_im, precision=HIGHEST_PREC) + jnp.einsum(
        "ab,...bc->...ac", left_im, part_re, precision=HIGHEST_PREC
    )
    out_re = jnp.einsum("...ab,cb->...ac", first_re, left_re, precision=HIGHEST_PREC) - jnp.einsum(
        "...ab,cb->...ac", first_im, left_im, precision=HIGHEST_PREC
    )
    out_im = jnp.einsum("...ab,cb->...ac", first_re, left_im, precision=HIGHEST_PREC) + jnp.einsum(
        "...ab,cb->...ac", first_im, left_re, precision=HIGHEST_PREC
    )
    return (out_re, out_im)


def position_terms(window, probe, amplitude, prop_re, prop_im, grad_scale):
    obj_re = window[:, None, 0]
    obj_im = window[:, None, 1]
    probe_re = probe[None, :, 0]
    probe_im = probe[None, :, 1]
    exit_re = probe_re * obj_re - probe_im * obj_im
    exit_im = probe_re * obj_im + probe_im * obj_re
    far_re, far_im = apply_both(prop_re, prop_im, exit_re, exit_im)
    intensity = jnp.sum(far_re * far_re + far_im * far_im, axis=1, keepdims=True)
    factor = (
        1.0 - amplitude[:, None].astype(jnp.float32) / jnp.maximum(jnp.sqrt(intensity), 1.0)
    ) * grad_scale
    back_re, back_im = apply_both(prop_re.T, -prop_im.T, far_re * factor, far_im * factor)
    obj_part_re = jnp.sum(probe_re * back_re + probe_im * back_im, axis=1)
    obj_part_im = jnp.sum(probe_re * back_im - probe_im * back_re, axis=1)
    probe_part_re = jnp.sum(obj_re * back_re + obj_im * back_im, axis=0)
    probe_part_im = jnp.sum(obj_re * back_im - obj_im * back_re, axis=0)
    return (
        jnp.stack([obj_part_re, obj_part_im], axis=1),
        jnp.stack([probe_part_re, probe_part_im], axis=1),
    )


def owner_of(strips, strip_owner):
    table = jnp.arange(strip_owner.shape[0], dtype=jnp.int32)
    return jnp.sum(jnp.where(strips[..., None] == table, strip_owner, 0), axis=-1)


def place_columns(strip_grad, start_cols, pieces):
    span_width = pieces.shape[-1]
    column_ids = start_cols[:, None] + jnp.arange(span_width, dtype=jnp.int32)[None, :]
    return strip_grad.at[:, :, column_ids].add(pieces.transpose(1, 2, 0, 3))


def per_device_general(object_field, probe, amplitude, offsets, strip_owner, chirp):
    tile_count = lax.axis_size("tile")
    pos_groups = lax.axis_size("pos")
    pos_count = amplitude.shape[0]
    win_size = probe.shape[-1]
    strip_rows = object_field.shape[1]
    width_all = object_field.shape[2]
    last_strip = tile_count - 1
    grad_scale = 1.0 / math.sqrt(pos_count * tile_count * pos_groups)
    prop_re, prop_im = build_propagator(chirp)
    everyone = lax.all_gather(offsets, "tile", axis=0, tiled=True)
    row_off = offsets[:, 0]
    strip_grad = jnp.zeros((2, strip_rows, width_all), jnp.float32)
    reach_strips = (win_size - 1) // strip_rows + 2
    flat_cols = everyone[:, 1]

    def cut_piece(start_col):
        return lax.dynamic_slice_in_dim(object_field, start_col, win_size, 2)

    pieces = jax.vmap(cut_piece)(flat_cols).reshape(tile_count, pos_count, 2, strip_rows, win_size)
    arrived = lax.all_to_all(pieces, "tile", split_axis=0, concat_axis=0, tiled=True)
    strip_of = row_off // strip_rows
    inside = row_off - strip_of * strip_rows
    strips = jnp.minimum(
        strip_of[:, None] + jnp.arange(reach_strips, dtype=jnp.int32)[None, :], last_strip
    )
    owners = owner_of(strips, strip_owner)
    slot_ids = jnp.arange(pos_count, dtype=jnp.int32)[:, None]
    stacked = (
        arrived[owners, slot_ids]
        .transpose(0, 2, 1, 3, 4)
        .reshape(pos_count, 2, reach_strips * strip_rows, win_size)
    )

    def cut_rows(stack_one, row_at):
        return lax.dynamic_slice_in_dim(stack_one, row_at, win_size, 1)

    windows = jax.vmap(cut_rows)(stacked, inside)
    obj_part, probe_sum = position_terms(
        windows.astype(jnp.float32), probe, amplitude, prop_re, prop_im, grad_scale
    )

    def put_rows(base_one, piece_one, row_at):
        return lax.dynamic_update_slice_in_dim(base_one, piece_one, row_at, 1)

    padded = jnp.zeros((pos_count, 2, reach_strips * strip_rows, win_size), jnp.float32)
    padded = jax.vmap(put_rows)(padded, obj_part, inside)
    split_grad = padded.reshape(pos_count, 2, reach_strips, strip_rows, win_size).transpose(
        0, 2, 1, 3, 4
    )
    outgoing = (
        jnp.zeros((tile_count, pos_count, 2, strip_rows, win_size), jnp.float32)
        .at[owners, slot_ids]
        .add(split_grad)
    )
    returned = lax.all_to_all(outgoing, "tile", split_axis=0, concat_axis=0, tiled=True)
    flat_back = returned.reshape(tile_count * pos_count, 2, strip_rows, win_size)
    strip_grad = place_columns(strip_grad, flat_cols, flat_back)
    strip_part = lax.psum_scatter(strip_grad, "pos", scatter_dimension=2, tiled=True)
    probe_total = lax.psum(probe_sum, ("tile", "pos"))
    row_share = win_size // pos_groups
    probe_out = lax.dynamic_slice_in_dim(
        probe_total, lax.axis_index("pos") * row_share, row_share, 2
    )
    return (strip_part, probe_out)


def strip_held(owner_ref, me, count):
    held = jnp.int32(0)
    for s in range(count):
        held = held + jnp.where(owner_ref[s] == me, s, 0).astype(jnp.int32)
    return held


def geometry(y_a, x_a, y_b, x_b):
    first = y_a < y_b
    return (
        jnp.where(first, y_a, y_b),
        jnp.where(first, x_a, x_b),
        jnp.where(first, x_b, x_a),
        first,
    )


def lane_iota(shape):
    return lax.broadcasted_iota(jnp.int32, shape, 1)


def row_iota(shape):
    return lax.broadcasted_iota(jnp.int32, shape, 0)


def pack_kernel(tiles, win, width, me_ref, owner_ref, *refs):
    offs = refs[:tiles]
    obj_ref = refs[tiles]
    outs = refs[tiles + 1 : 2 * tiles + 1]
    buf, pack, params, in_sem, out_sem = refs[2 * tiles + 1 :]
    half = win // 2
    quarter = win // 4
    strip = strip_held(owner_ref, me_ref[0], tiles)

    def fetch(k):
        start = pl.multiple_of(params[k, 3], 128)
        return pltpu.make_async_copy(
            obj_ref.at[:, :, pl.ds(start, 2 * win)], buf.at[k], in_sem.at[k]
        )

    for k in range(tiles):
        y_up, x_up, x_low, _ = geometry(offs[k][0, 0], offs[k][0, 1], offs[k][1, 0], offs[k][1, 1])
        left = jnp.minimum(x_up, x_low)
        params[k, 0] = y_up
        params[k, 1] = (x_low > x_up).astype(jnp.int32)
        params[k, 3] = jnp.minimum((left // 128) * 128, width - 2 * win)
        params[k, 2] = left - params[k, 3]
        fetch(k).start()

    def one(k, carry):
        fetch(k).wait()
        y_up = params[k, 0]
        right = params[k, 1]
        rem = params[k, 2]
        turn = lax.rem(half - rem, half)
        keep = lane_iota((quarter, half)) < half - rem
        base = strip * win
        for part in range(2):
            for chunk in range(2):
                outer = []
                for level in range(2):
                    row0 = level * half + chunk * quarter
                    wide = buf[k, part, row0 : row0 + quarter, :].astype(jnp.float32)
                    spun = [
                        pltpu.roll(wide[:, half * b : half * (b + 1)], turn, 1) for b in range(4)
                    ]
                    cols = [jnp.where(keep, spun[b], spun[b + 1]) for b in range(3)]
                    rows = base + row0 + row_iota((quarter, half))
                    in_upper = (rows < y_up + win).astype(jnp.int32)
                    low_first = in_upper == right
                    pack[k, part, row0 : row0 + quarter, 0:half] = jnp.where(
                        low_first, cols[0], cols[1]
                    ).astype(pack.dtype)
                    pack[k, part, row0 : row0 + quarter, half:win] = jnp.where(
                        low_first, cols[1], cols[2]
                    ).astype(pack.dtype)
                    outer.append(jnp.where(right == 1, cols[2], cols[0]))
                high = base + half + chunk * quarter + row_iota((quarter, half))
                use_high = (high >= y_up + half) & (high < y_up + win)
                pack[k, part, win : win + quarter, half * chunk : half * (chunk + 1)] = jnp.where(
                    use_high, outer[1], outer[0]
                ).astype(pack.dtype)
        return carry

    for k in range(tiles):
        one(k, 0)
        pltpu.make_async_copy(pack.at[k], outs[k], out_sem.at[k]).start()
    for k in range(tiles):
        pltpu.make_async_copy(pack.at[k], outs[k], out_sem.at[k]).wait()


def halves(x):
    high = x.astype(jnp.bfloat16)
    return high, (x - high.astype(jnp.float32)).astype(jnp.bfloat16)


def dot(a, b):
    return lax.dot_general(a, b, (((1,), (0,)), ((), ())), preferred_element_type=jnp.float32)


def rows_from(ref, part, start, count):
    down = pl.multiple_of((start // 8) * 8, 8)
    rows = ref[part, pl.ds(down, count + 8), :]
    return pltpu.roll(rows, lax.rem(count + 8 - (start - down), count + 8), 0)[0:count]


def rows_to(ref, part, start, blocks):
    down = pl.multiple_of((start // 8) * 8, 8)
    rows = jnp.concatenate(blocks + [jnp.zeros((8, blocks[0].shape[1]), jnp.float32)], axis=0)
    ref[part, pl.ds(down, rows.shape[0]), :] = pltpu.roll(rows, start - down, 0)


LEVELS = 32600.0
CODE_UNIT = 256.0


def code_of(peak):
    return jnp.ceil(jnp.log(jnp.maximum(peak, 1e-30)) * (CODE_UNIT / math.log(2.0)))


def step_of(code):
    return jnp.exp(code * (math.log(2.0) / CODE_UNIT)) * (1.0 / LEVELS)


def column_peak(x):
    return jnp.max(jnp.abs(x), axis=0, keepdims=True)


def to_levels(x, code):
    return jnp.floor(x * (1.0 / step_of(code)) + 0.5).astype(jnp.int32).astype(jnp.int16)


def code_rows(codes):
    rest = jnp.zeros((16 - len(codes), codes[0].shape[1]), jnp.float32)
    return jnp.concatenate(codes + [rest], axis=0).astype(jnp.int32).astype(jnp.int16)


def wide_of(x):
    return x.astype(jnp.int32).astype(jnp.float32)


def compute_kernel(tiles, pos_groups, win, modes, grad_scale, me_ref, owner_ref, off_ref, *refs):
    packs = refs[:tiles]
    probe, amp, prop_re, prop_im, prop_t_re, prop_t_im, spot_ref = refs[tiles : tiles + 7]
    grads = refs[tiles + 7 : 2 * tiles + 7]
    away_ref, kept_ref = refs[2 * tiles + 7 : 2 * tiles + 9]
    (
        held, cat, wins, far, factor, right_a, right_b, left_a, left_b, obj_acc, probe_acc, gcat, outer_acc, gpack,
        in_sem, out_sem, piece_sem,
    ) = refs[2 * tiles + 9 :]
    half = win // 2
    quarter = win // 4
    me = me_ref[0]
    fetches = [pltpu.make_async_copy(packs[k], held.at[k], in_sem.at[k]) for k in range(tiles)]
    for fetch in fetches:
        fetch.start()

    for way in range(2):
        if way == 0:
            r_re, r_im = prop_t_re[...], prop_t_im[...]
            l_re, l_im = prop_re[...], prop_im[...]
        else:
            r_re, r_im = prop_re[...], -prop_im[...]
            l_re, l_im = prop_t_re[...], -prop_t_im[...]
        (rr, rr_low), (ri, ri_low) = halves(r_re), halves(r_im)
        for row, (a, b) in enumerate([(rr, ri), (rr, ri), (-ri, rr), (-ri, rr)]):
            right_a[way, row * win : (row + 1) * win, 0:win] = a
            right_a[way, row * win : (row + 1) * win, win : 2 * win] = b
        for row, (a, b) in enumerate([(rr_low, ri_low), (-ri_low, rr_low)]):
            right_b[way, row * win : (row + 1) * win, 0:win] = a
            right_b[way, row * win : (row + 1) * win, win : 2 * win] = b
        (lr, lr_low), (li, li_low) = halves(l_re), halves(l_im)
        for col, (a, b) in enumerate([(lr, li), (lr, li), (-li, lr), (-li, lr)]):
            left_a[way, 0:win, col * win : (col + 1) * win] = a
            left_a[way, win : 2 * win, col * win : (col + 1) * win] = b
        for col, (a, b) in enumerate([(lr_low, li_low), (-li_low, lr_low)]):
            left_b[way, 0:win, col * win : (col + 1) * win] = a
            left_b[way, win : 2 * win, col * win : (col + 1) * win] = b

    y_up, x_up, x_low, first = geometry(off_ref[0, 0], off_ref[0, 1], off_ref[1, 0], off_ref[1, 1])
    right = x_low > x_up
    strip = y_up // win
    rem = y_up - strip * win
    low_rem = lax.rem(rem, half)
    mid_block = (y_up + half) // half

    def slot_of(s):
        return lax.rem(me - owner_ref[jnp.minimum(s, tiles - 1)] + tiles, tiles)

    for fetch in fetches:
        fetch.wait()
    slots = [slot_of(strip + d) for d in range(3)]
    for part in range(2):
        for d in range(3):
            cat[part, d * win : (d + 1) * win, :] = held[slots[d], part, 0:win, :].astype(jnp.float32)
        for d in range(2):
            slot = slot_of((mid_block + d) // 2)
            for chunk in range(2):
                outer_acc[part, d * half + chunk * quarter : d * half + (chunk + 1) * quarter, :] = held[
                    slot, part, win : win + quarter, half * chunk : half * (chunk + 1)
                ].astype(jnp.float32)
    for part in range(2):
        upper = rows_from(cat, part, rem, win)
        wins[0, part] = upper
        wins[1, part, half:win, :] = rows_from(cat, part, rem + win, half)
        outer = rows_from(outer_acc, part, low_rem, half)
        wins[1, part, 0:half, 0:half] = jnp.where(right, upper[half:win, half:win], outer)
        wins[1, part, 0:half, half:win] = jnp.where(right, outer, upper[half:win, 0:half])

    def both(way, re, im):
        (re_h, re_l), (im_h, im_l) = halves(re), halves(im)
        mid = dot(jnp.concatenate([re_h, re_l, im_h, im_l], axis=1), right_a[way]) + dot(
            jnp.concatenate([re_h, im_h], axis=1), right_b[way]
        )
        (re_h, re_l), (im_h, im_l) = halves(mid[:, 0:win]), halves(mid[:, win : 2 * win])
        return dot(left_a[way], jnp.concatenate([re_h, re_l, im_h, im_l], axis=0)) + dot(
            left_b[way], jnp.concatenate([re_h, im_h], axis=0)
        )

    def forward(n, carry):
        q = n // modes
        m = lax.rem(n, modes)
        p_re, p_im = probe[m, 0], probe[m, 1]
        w_re, w_im = wins[q, 0], wins[q, 1]
        far[n] = both(0, p_re * w_re - p_im * w_im, p_re * w_im + p_im * w_re)
        return carry

    lax.fori_loop(0, 2 * modes, forward, 0)
    for q in range(2):
        total = jnp.zeros((win, win), jnp.float32)
        for m in range(modes):
            f_re, f_im = far[q * modes + m, 0:win, :], far[q * modes + m, win : 2 * win, :]
            total = total + (f_re * f_re + f_im * f_im)
        frame = jnp.where(first, q, 1 - q)
        measured = amp[frame].astype(jnp.float32)
        factor[q] = (1.0 - measured / jnp.maximum(jnp.sqrt(total), 1.0)) * grad_scale
    obj_acc[...] = jnp.zeros_like(obj_acc)
    probe_acc[...] = jnp.zeros_like(probe_acc)

    def backward(n, carry):
        q = n // modes
        m = lax.rem(n, modes)
        scale = factor[q]
        back = both(1, far[n, 0:win, :] * scale, far[n, win : 2 * win, :] * scale)
        b_re, b_im = back[0:win, :], back[win : 2 * win, :]
        p_re, p_im = probe[m, 0], probe[m, 1]
        w_re, w_im = wins[q, 0], wins[q, 1]
        obj_acc[q, 0] = obj_acc[q, 0] + (p_re * b_re + p_im * b_im)
        obj_acc[q, 1] = obj_acc[q, 1] + (p_re * b_im - p_im * b_re)
        probe_acc[m, 0] = probe_acc[m, 0] + (w_re * b_re + w_im * b_im)
        probe_acc[m, 1] = probe_acc[m, 1] + (w_re * b_im - w_im * b_re)
        return carry

    lax.fori_loop(0, 2 * modes, backward, 0)
    share = win // pos_groups
    spot = spot_ref[0]
    piece_copies = []
    for j in range(pos_groups):
        start = pl.multiple_of(jnp.bitwise_xor(spot, j) * share, share)
        home = (away_ref if j % 2 else kept_ref).at[j // 2]
        piece_copies.append(
            pltpu.make_async_copy(probe_acc.at[:, :, pl.ds(start, share), :], home, piece_sem.at[j])
        )
        piece_copies[-1].start()

    gcat[...] = jnp.zeros_like(gcat)
    outer_acc[...] = jnp.zeros_like(outer_acc)
    for part in range(2):
        low_a = obj_acc[1, part, 0:half, 0:half]
        low_b = obj_acc[1, part, 0:half, half:win]
        zero = jnp.zeros_like(low_a)
        obj_acc[0, part, half:win, 0:half] += jnp.where(right, zero, low_b)
        obj_acc[0, part, half:win, half:win] += jnp.where(right, low_a, zero)
        rows_to(gcat, part, rem, [obj_acc[0, part], obj_acc[1, part, half:win, :]])
        rows_to(outer_acc, part, low_rem, [jnp.where(right, low_b, low_a)])
        outer = outer_acc[part, 0:half, :] + outer_acc[part, half:win, :]
        outer_code = code_of(column_peak(outer))
        outer_levels = to_levels(outer, outer_code)
        for d in range(3):
            codes = []
            for level in range(2):
                rows = gcat[part, d * win + level * half : d * win + (level + 1) * half, :]
                codes.append(code_of(column_peak(rows)))
                gpack[d, part, level * half : (level + 1) * half, :] = to_levels(rows, codes[-1])
            for chunk in range(2):
                gpack[d, part, win : win + quarter, half * chunk : half * (chunk + 1)] = outer_levels[
                    chunk * quarter : (chunk + 1) * quarter, :
                ]
            codes.append(jnp.concatenate([outer_code, outer_code], axis=1))
            gpack[d, part, win + quarter : win + quarter + 16, :] = code_rows(codes)
    grad_copies = []
    for k in range(tiles):
        there = strip_held(owner_ref, lax.rem(me + k, tiles), tiles)
        d = jnp.clip(there - strip, 0, 2)
        grad_copies.append(pltpu.make_async_copy(gpack.at[d], grads[k], out_sem.at[k]))
        grad_copies[-1].start()
    for copy in piece_copies + grad_copies:
        copy.wait()


def probe_pack_kernel(blocks, rows, kept_ref, came_ref, total_ref, pack_ref):
    codes = []
    for b in range(blocks):
        total = kept_ref[b] + came_ref[b]
        total_ref[b] = total
        codes.append(code_of(column_peak(total)))
        pack_ref[b * rows : (b + 1) * rows, :] = to_levels(total, codes[-1])
    pack_ref[blocks * rows : blocks * rows + 16, :] = code_rows(codes)


def place_kernel(tiles, pos_groups, win, slab, me_ref, spot_ref, owner_ref, *refs):
    count = tiles * pos_groups
    offs = refs[:pos_groups]
    packs = refs[pos_groups : pos_groups + count]
    probe_own = refs[pos_groups + count]
    probe_packs = refs[pos_groups + count + 1 : pos_groups + count + tiles]
    out_ref, probe_ref = refs[pos_groups + count + tiles : pos_groups + count + tiles + 2]
    held, acc, params, in_sem, out_sem = refs[pos_groups + count + tiles + 2 :]
    half = win // 2
    quarter = win // 4
    me = me_ref[0]
    strip = strip_held(owner_ref, me, tiles)
    base = strip * win
    first_col = spot_ref[0] * slab
    margin = 2 * win
    span = 3 * half
    for n in range(count):
        j, k = n // tiles, n % tiles
        off = offs[j]
        y_up, x_up, x_low, _ = geometry(off[2 * k, 0], off[2 * k, 1], off[2 * k + 1, 0], off[2 * k + 1, 1])
        left = jnp.minimum(x_up, x_low)
        hit = (y_up < base + win) & (y_up + span > base) & (left < first_col + slab) & (left + span > first_col)
        params[n, 0] = hit.astype(jnp.int32)
        params[n, 1] = y_up
        params[n, 2] = (x_low > x_up).astype(jnp.int32)
        params[n, 3] = left - first_col + margin

        @pl.when(hit)
        def _():
            pltpu.make_async_copy(packs[n], held.at[n], in_sem.at[n]).start()

    def clear(i, carry):
        acc[:, pl.ds(pl.multiple_of(i * 8, 8), 8), :] = jnp.zeros((2, 8, acc.shape[2]), jnp.float32)
        return carry

    lax.fori_loop(0, win // 8, clear, 0)
    blocks, rows_each = probe_own.shape[0], probe_own.shape[1]
    scales = [step_of(wide_of(pk[blocks * rows_each : blocks * rows_each + 16, :])) for pk in probe_packs]
    for b in range(blocks):
        total = probe_own[b]
        for pk, scale in zip(probe_packs, scales):
            total = total + wide_of(pk[b * rows_each : (b + 1) * rows_each, :]) * scale[b : b + 1, :]
        probe_ref[b] = total

    def one(n, carry):
        @pl.when(params[n, 0] == 1)
        def _():
            pltpu.make_async_copy(packs[0], held.at[n], in_sem.at[n]).wait()
            y_up = params[n, 1]
            right = params[n, 2]
            col = params[n, 3]
            start = pl.multiple_of((col // 128) * 128, 128)
            rem = col - start
            lanes = lane_iota((quarter, half))
            stay = lanes >= rem

            for part in range(2):
                steps = step_of(wide_of(held[n, part, win + quarter : win + quarter + 16, :]))
                for chunk in range(4):
                    row0 = chunk * quarter
                    level = chunk // 2
                    rows = base + row0 + row_iota((quarter, half))
                    low_first = (rows < y_up + win).astype(jnp.int32) == right
                    in_outer = (rows >= y_up + half) & (rows < y_up + win)
                    main = wide_of(held[n, part, row0 : row0 + quarter, :]) * steps[level : level + 1, :]
                    m0 = main[:, 0:half]
                    m1 = main[:, half:win]
                    side = held[n, part, win : win + quarter, half * (chunk % 2) : half * (chunk % 2 + 1)]
                    side = jnp.where(in_outer, wide_of(side) * steps[2:3, 0:half], 0.0)
                    cols = [
                        jnp.where(low_first, m0, jnp.where(right == 0, side, 0.0)),
                        jnp.where(low_first, m1, m0),
                        jnp.where(low_first, jnp.where(right == 1, side, 0.0), m1),
                    ]
                    spun = [pltpu.roll(c, rem, 1) for c in cols]
                    zero = jnp.zeros_like(m0)
                    shifted = [
                        jnp.where(stay, spun[0], zero),
                        jnp.where(stay, spun[1], spun[0]),
                        jnp.where(stay, spun[2], spun[1]),
                        jnp.where(stay, zero, spun[2]),
                    ]
                    for b in range(4):
                        at = pl.ds(pl.multiple_of(start + b * half, 128), half)
                        acc[part, row0 : row0 + quarter, at] += shifted[b]

        return carry

    lax.fori_loop(0, count, one, 0)
    out = pltpu.make_async_copy(acc.at[:, :, margin : margin + slab], out_ref, out_sem)
    out.start()
    out.wait()


def shifted(x, axis, count, k):
    return lax.ppermute(x, axis, [(i, (i + k) % count) for i in range(count)])


def swapped(x, axis, count, bit):
    return lax.ppermute(x, axis, [(i, i ^ bit) for i in range(count)])


def per_device_packed(object_field, probe, amplitude, offsets, strip_owner, chirp):
    tiles = lax.axis_size("tile")
    pos_groups = lax.axis_size("pos")
    pos_count, win, _ = amplitude.shape
    modes = probe.shape[0]
    width = object_field.shape[2]
    slab = width // pos_groups
    half = win // 2
    quarter = win // 4
    grad_scale = 1.0 / math.sqrt(pos_count * tiles * pos_groups)
    me = lax.axis_index("tile").astype(jnp.int32).reshape(1)
    spot = lax.axis_index("pos").astype(jnp.int32).reshape(1)
    smem = pl.BlockSpec(memory_space=pltpu.SMEM)
    vmem = pl.BlockSpec(memory_space=pltpu.VMEM)
    anywhere = pl.BlockSpec(memory_space=pl.ANY)
    pack_shape = (2, win + quarter, win)
    grad_shape = (2, win + quarter + 16, win)
    share = win // pos_groups

    offs = [offsets] + [shifted(offsets, "tile", tiles, tiles - k) for k in range(1, tiles)]
    packs = pl.pallas_call(
        functools.partial(pack_kernel, tiles, win, width),
        out_shape=[jax.ShapeDtypeStruct(pack_shape, jnp.bfloat16)] * tiles,
        in_specs=[smem] * (2 + tiles) + [anywhere],
        out_specs=[anywhere] * tiles,
        scratch_shapes=[
            pltpu.VMEM((tiles, 2, win, 2 * win), jnp.bfloat16),
            pltpu.VMEM((tiles,) + pack_shape, jnp.bfloat16),
            pltpu.SMEM((tiles, 4), jnp.int32),
            pltpu.SemaphoreType.DMA((tiles,)),
            pltpu.SemaphoreType.DMA((tiles,)),
        ],
        name="pack",
    )(me, strip_owner, *offs, object_field)
    arrived = [packs[0]] + [shifted(packs[k], "tile", tiles, k) for k in range(1, tiles)]
    prop_re, prop_im = build_propagator(chirp)
    results = pl.pallas_call(
        functools.partial(compute_kernel, tiles, pos_groups, win, modes, grad_scale),
        out_shape=[jax.ShapeDtypeStruct(grad_shape, jnp.int16)] * tiles
        + [jax.ShapeDtypeStruct((pos_groups // 2, modes, 2, share, win), jnp.float32)] * 2,
        in_specs=[smem] * 3 + [anywhere] * tiles + [vmem] * 6 + [smem],
        out_specs=[anywhere] * (tiles + 2),
        scratch_shapes=[
            pltpu.VMEM((tiles,) + pack_shape, jnp.bfloat16),
            pltpu.VMEM((2, 3 * win, win), jnp.float32),
            pltpu.VMEM((2, 2, win, win), jnp.float32),
            pltpu.VMEM((2 * modes, 2 * win, win), jnp.float32),
            pltpu.VMEM((2, win, win), jnp.float32),
            pltpu.VMEM((2, 4 * win, 2 * win), jnp.bfloat16),
            pltpu.VMEM((2, 2 * win, 2 * win), jnp.bfloat16),
            pltpu.VMEM((2, 2 * win, 4 * win), jnp.bfloat16),
            pltpu.VMEM((2, 2 * win, 2 * win), jnp.bfloat16),
            pltpu.VMEM((2, 2, win, win), jnp.float32),
            pltpu.VMEM((modes, 2, win, win), jnp.float32),
            pltpu.VMEM((2, 3 * win, win), jnp.float32),
            pltpu.VMEM((2, win, half), jnp.float32),
            pltpu.VMEM((3,) + grad_shape, jnp.int16),
            pltpu.SemaphoreType.DMA((tiles,)),
            pltpu.SemaphoreType.DMA((tiles,)),
            pltpu.SemaphoreType.DMA((pos_groups,)),
        ],
        name="propagate",
    )(me, strip_owner, offsets, *arrived, probe, amplitude, prop_re, prop_im, prop_re.T, prop_im.T, spot)
    grads, (away, kept) = results[:tiles], results[tiles:]

    column = [grads[0]] + [shifted(grads[k], "tile", tiles, k) for k in range(1, tiles)]
    column_offs = [jnp.concatenate([offs[(tiles - k) % tiles] for k in range(tiles)], axis=0)]
    columns = [column]
    bit = pos_groups // 2
    while bit:
        columns = columns + [[swapped(x, "pos", pos_groups, bit) for x in c] for c in columns]
        column_offs = column_offs + [swapped(o, "pos", pos_groups, bit) for o in column_offs]
        bit //= 2

    kept = kept + swapped(away, "pos", pos_groups, 1)
    bit = 2
    while kept.shape[0] > 2:
        kept = kept[0::2] + swapped(kept[1::2], "pos", pos_groups, bit)
        bit *= 2
    blocks = modes * 2
    came = swapped(kept[1], "pos", pos_groups, bit)
    probe_own, probe_pack = pl.pallas_call(
        functools.partial(probe_pack_kernel, blocks, share),
        out_shape=[
            jax.ShapeDtypeStruct((blocks, share, win), jnp.float32),
            jax.ShapeDtypeStruct((blocks * share + 16, win), jnp.int16),
        ],
        name="probe_pack",
    )(kept[0].reshape(blocks, share, win), came.reshape(blocks, share, win))
    probe_packs = [shifted(probe_pack, "tile", tiles, k) for k in range(1, tiles)]

    flat = [x for c in columns for x in c]
    count = len(flat)
    strip_part, probe_out = pl.pallas_call(
        functools.partial(place_kernel, tiles, pos_groups, win, slab),
        out_shape=[
            jax.ShapeDtypeStruct((2, win, slab), jnp.float32),
            jax.ShapeDtypeStruct((blocks, share, win), jnp.float32),
        ],
        in_specs=[smem] * (3 + pos_groups) + [anywhere] * count + [vmem] * tiles,
        out_specs=[anywhere, vmem],
        scratch_shapes=[
            pltpu.VMEM((count,) + grad_shape, jnp.int16),
            pltpu.VMEM((2, win, slab + 4 * win), jnp.float32),
            pltpu.SMEM((count, 4), jnp.int32),
            pltpu.SemaphoreType.DMA((count,)),
            pltpu.SemaphoreType.DMA,
        ],
        name="place",
    )(me, spot, strip_owner, *column_offs, *flat, probe_own, *probe_packs)
    return (strip_part, probe_out.reshape(modes, 2, share, win))


def per_device(object_field, probe, amplitude, offsets, strip_owner, chirp):
    tiles = lax.axis_size("tile")
    pos_groups = lax.axis_size("pos")
    pos_count, win, _ = amplitude.shape
    width = object_field.shape[2]
    packed = (
        pos_count == 2
        and object_field.shape[1] == win
        and win == 256
        and pos_groups & (pos_groups - 1) == 0
        and width // pos_groups >= 2 * win
        and (width // pos_groups) % 128 == 0
        and pos_groups >= 4
        and (win // pos_groups) % 16 == 0
    )
    plan = per_device_packed if packed else per_device_general
    return plan(object_field, probe, amplitude, offsets, strip_owner, chirp)


def solution(mesh):
    return jax.shard_map(
        per_device,
        mesh=mesh,
        in_specs=(
            P(None, ("groups", "tile"), None),
            P("groups", None, None, None),
            P(("groups", "tile", "pos"), None, None),
            P(("groups", "tile", "pos"), None),
            P("groups"),
            P(),
        ),
        out_specs=(P(None, ("groups", "tile"), "pos"), P("groups", None, "pos", None)),
        check_vma=False,
    )
```

```python
import functools
import math

import jax
import jax.numpy as jnp
from jax import lax
from jax.experimental import pallas as pl
from jax.experimental.pallas import tpu as pltpu
from jax.sharding import PartitionSpec as P


HIGHEST_PREC = lax.Precision.HIGHEST


def build_propagator(chirp):
    win_size = chirp.shape[0]
    freq_index = jnp.arange(win_size, dtype=jnp.int32)
    phase_grid = (
        2.0
        * math.pi
        / win_size
        * (freq_index[:, None] * freq_index[None, :] % win_size).astype(jnp.float32)
    )
    unit_norm = 1.0 / math.sqrt(win_size)
    fourier_re = jnp.cos(phase_grid) * unit_norm
    fourier_im = -jnp.sin(phase_grid) * unit_norm
    chirp_re = jnp.cos(chirp)[:, None]
    chirp_im = jnp.sin(chirp)[:, None]
    middle_re = chirp_re * fourier_re - chirp_im * fourier_im
    middle_im = chirp_re * fourier_im + chirp_im * fourier_re
    prop_re = jnp.dot(fourier_re, middle_re, precision=HIGHEST_PREC) + jnp.dot(
        fourier_im, middle_im, precision=HIGHEST_PREC
    )
    prop_im = jnp.dot(fourier_re, middle_im, precision=HIGHEST_PREC) - jnp.dot(
        fourier_im, middle_re, precision=HIGHEST_PREC
    )
    return (prop_re, prop_im)


def apply_both(left_re, left_im, part_re, part_im):
    first_re = jnp.einsum("ab,...bc->...ac", left_re, part_re, precision=HIGHEST_PREC) - jnp.einsum(
        "ab,...bc->...ac", left_im, part_im, precision=HIGHEST_PREC
    )
    first_im = jnp.einsum("ab,...bc->...ac", left_re, part_im, precision=HIGHEST_PREC) + jnp.einsum(
        "ab,...bc->...ac", left_im, part_re, precision=HIGHEST_PREC
    )
    out_re = jnp.einsum("...ab,cb->...ac", first_re, left_re, precision=HIGHEST_PREC) - jnp.einsum(
        "...ab,cb->...ac", first_im, left_im, precision=HIGHEST_PREC
    )
    out_im = jnp.einsum("...ab,cb->...ac", first_re, left_im, precision=HIGHEST_PREC) + jnp.einsum(
        "...ab,cb->...ac", first_im, left_re, precision=HIGHEST_PREC
    )
    return (out_re, out_im)


def position_terms(window, probe, amplitude, prop_re, prop_im, grad_scale):
    obj_re = window[:, None, 0]
    obj_im = window[:, None, 1]
    probe_re = probe[None, :, 0]
    probe_im = probe[None, :, 1]
    exit_re = probe_re * obj_re - probe_im * obj_im
    exit_im = probe_re * obj_im + probe_im * obj_re
    far_re, far_im = apply_both(prop_re, prop_im, exit_re, exit_im)
    intensity = jnp.sum(far_re * far_re + far_im * far_im, axis=1, keepdims=True)
    factor = (
        1.0 - amplitude[:, None].astype(jnp.float32) / jnp.maximum(jnp.sqrt(intensity), 1.0)
    ) * grad_scale
    back_re, back_im = apply_both(prop_re.T, -prop_im.T, far_re * factor, far_im * factor)
    obj_part_re = jnp.sum(probe_re * back_re + probe_im * back_im, axis=1)
    obj_part_im = jnp.sum(probe_re * back_im - probe_im * back_re, axis=1)
    probe_part_re = jnp.sum(obj_re * back_re + obj_im * back_im, axis=0)
    probe_part_im = jnp.sum(obj_re * back_im - obj_im * back_re, axis=0)
    return (
        jnp.stack([obj_part_re, obj_part_im], axis=1),
        jnp.stack([probe_part_re, probe_part_im], axis=1),
    )


def owner_of(strips, strip_owner):
    table = jnp.arange(strip_owner.shape[0], dtype=jnp.int32)
    return jnp.sum(jnp.where(strips[..., None] == table, strip_owner, 0), axis=-1)


def place_columns(strip_grad, start_cols, pieces):
    span_width = pieces.shape[-1]
    column_ids = start_cols[:, None] + jnp.arange(span_width, dtype=jnp.int32)[None, :]
    return strip_grad.at[:, :, column_ids].add(pieces.transpose(1, 2, 0, 3))


def per_device_general(object_field, probe, amplitude, offsets, strip_owner, chirp):
    tile_count = lax.axis_size("tile")
    pos_groups = lax.axis_size("pos")
    pos_count = amplitude.shape[0]
    win_size = probe.shape[-1]
    strip_rows = object_field.shape[1]
    width_all = object_field.shape[2]
    last_strip = tile_count - 1
    grad_scale = 1.0 / math.sqrt(pos_count * tile_count * pos_groups)
    prop_re, prop_im = build_propagator(chirp)
    everyone = lax.all_gather(offsets, "tile", axis=0, tiled=True)
    row_off = offsets[:, 0]
    strip_grad = jnp.zeros((2, strip_rows, width_all), jnp.float32)
    reach_strips = (win_size - 1) // strip_rows + 2
    flat_cols = everyone[:, 1]

    def cut_piece(start_col):
        return lax.dynamic_slice_in_dim(object_field, start_col, win_size, 2)

    pieces = jax.vmap(cut_piece)(flat_cols).reshape(tile_count, pos_count, 2, strip_rows, win_size)
    arrived = lax.all_to_all(pieces, "tile", split_axis=0, concat_axis=0, tiled=True)
    strip_of = row_off // strip_rows
    inside = row_off - strip_of * strip_rows
    strips = jnp.minimum(
        strip_of[:, None] + jnp.arange(reach_strips, dtype=jnp.int32)[None, :], last_strip
    )
    owners = owner_of(strips, strip_owner)
    slot_ids = jnp.arange(pos_count, dtype=jnp.int32)[:, None]
    stacked = (
        arrived[owners, slot_ids]
        .transpose(0, 2, 1, 3, 4)
        .reshape(pos_count, 2, reach_strips * strip_rows, win_size)
    )

    def cut_rows(stack_one, row_at):
        return lax.dynamic_slice_in_dim(stack_one, row_at, win_size, 1)

    windows = jax.vmap(cut_rows)(stacked, inside)
    obj_part, probe_sum = position_terms(
        windows.astype(jnp.float32), probe, amplitude, prop_re, prop_im, grad_scale
    )

    def put_rows(base_one, piece_one, row_at):
        return lax.dynamic_update_slice_in_dim(base_one, piece_one, row_at, 1)

    padded = jnp.zeros((pos_count, 2, reach_strips * strip_rows, win_size), jnp.float32)
    padded = jax.vmap(put_rows)(padded, obj_part, inside)
    split_grad = padded.reshape(pos_count, 2, reach_strips, strip_rows, win_size).transpose(
        0, 2, 1, 3, 4
    )
    outgoing = (
        jnp.zeros((tile_count, pos_count, 2, strip_rows, win_size), jnp.float32)
        .at[owners, slot_ids]
        .add(split_grad)
    )
    returned = lax.all_to_all(outgoing, "tile", split_axis=0, concat_axis=0, tiled=True)
    flat_back = returned.reshape(tile_count * pos_count, 2, strip_rows, win_size)
    strip_grad = place_columns(strip_grad, flat_cols, flat_back)
    strip_part = lax.psum_scatter(strip_grad, "pos", scatter_dimension=2, tiled=True)
    probe_total = lax.psum(probe_sum, ("tile", "pos"))
    row_share = win_size // pos_groups
    probe_out = lax.dynamic_slice_in_dim(
        probe_total, lax.axis_index("pos") * row_share, row_share, 2
    )
    return (strip_part, probe_out)


def strip_held(owner_ref, me, count):
    held = jnp.int32(0)
    for s in range(count):
        held = held + jnp.where(owner_ref[s] == me, s, 0).astype(jnp.int32)
    return held


def geometry(y_a, x_a, y_b, x_b):
    first = y_a < y_b
    return (
        jnp.where(first, y_a, y_b),
        jnp.where(first, x_a, x_b),
        jnp.where(first, x_b, x_a),
        first,
    )


def lane_iota(shape):
    return lax.broadcasted_iota(jnp.int32, shape, 1)


def row_iota(shape):
    return lax.broadcasted_iota(jnp.int32, shape, 0)


def pack_kernel(tiles, asked, win, width, me_ref, owner_ref, *refs):
    offs = refs[:asked]
    obj_ref = refs[asked]
    outs = refs[asked + 1 : 2 * asked + 1]
    buf, pack, params, in_sem, out_sem = refs[2 * asked + 1 :]
    half = win // 2
    quarter = win // 4
    strip = strip_held(owner_ref, me_ref[0], tiles)

    def fetch(k):
        start = pl.multiple_of(params[k, 3], 128)
        return pltpu.make_async_copy(
            obj_ref.at[:, :, pl.ds(start, 2 * win)], buf.at[k], in_sem.at[k]
        )

    for k in range(asked):
        y_up, x_up, x_low, _ = geometry(offs[k][0, 0], offs[k][0, 1], offs[k][1, 0], offs[k][1, 1])
        left = jnp.minimum(x_up, x_low)
        params[k, 0] = y_up
        params[k, 1] = (x_low > x_up).astype(jnp.int32)
        params[k, 3] = jnp.minimum((left // 128) * 128, width - 2 * win)
        params[k, 2] = left - params[k, 3]
        fetch(k).start()

    def one(k, carry):
        fetch(k).wait()
        y_up = params[k, 0]
        right = params[k, 1]
        rem = params[k, 2]
        turn = lax.rem(half - rem, half)
        keep = lane_iota((quarter, half)) < half - rem
        base = strip * win
        for part in range(2):
            for chunk in range(2):
                outer = []
                for level in range(2):
                    row0 = level * half + chunk * quarter
                    wide = buf[k, part, row0 : row0 + quarter, :].astype(jnp.float32)
                    spun = [
                        pltpu.roll(wide[:, half * b : half * (b + 1)], turn, 1) for b in range(4)
                    ]
                    cols = [jnp.where(keep, spun[b], spun[b + 1]) for b in range(3)]
                    rows = base + row0 + row_iota((quarter, half))
                    in_upper = (rows < y_up + win).astype(jnp.int32)
                    low_first = in_upper == right
                    pack[k, part, row0 : row0 + quarter, 0:half] = jnp.where(
                        low_first, cols[0], cols[1]
                    ).astype(pack.dtype)
                    pack[k, part, row0 : row0 + quarter, half:win] = jnp.where(
                        low_first, cols[1], cols[2]
                    ).astype(pack.dtype)
                    outer.append(jnp.where(right == 1, cols[2], cols[0]))
                high = base + half + chunk * quarter + row_iota((quarter, half))
                use_high = (high >= y_up + half) & (high < y_up + win)
                pack[k, part, win : win + quarter, half * chunk : half * (chunk + 1)] = jnp.where(
                    use_high, outer[1], outer[0]
                ).astype(pack.dtype)
        return carry

    for k in range(asked):
        one(k, 0)
        pltpu.make_async_copy(pack.at[k], outs[k], out_sem.at[k]).start()
    for k in range(asked):
        pltpu.make_async_copy(pack.at[k], outs[k], out_sem.at[k]).wait()


def halves(x):
    high = x.astype(jnp.bfloat16)
    return high, (x - high.astype(jnp.float32)).astype(jnp.bfloat16)


def dot(a, b):
    return lax.dot_general(a, b, (((1,), (0,)), ((), ())), preferred_element_type=jnp.float32)


def rows_from(ref, part, start, count):
    down = pl.multiple_of((start // 8) * 8, 8)
    rows = ref[part, pl.ds(down, count + 8), :]
    return pltpu.roll(rows, lax.rem(count + 8 - (start - down), count + 8), 0)[0:count]


def rows_to(ref, part, start, blocks):
    down = pl.multiple_of((start // 8) * 8, 8)
    rows = jnp.concatenate(blocks + [jnp.zeros((8, blocks[0].shape[1]), jnp.float32)], axis=0)
    ref[part, pl.ds(down, rows.shape[0]), :] = pltpu.roll(rows, start - down, 0)


LEVELS = 32600.0
CODE_UNIT = 256.0


def code_of(peak):
    return jnp.ceil(jnp.log(jnp.maximum(peak, 1e-30)) * (CODE_UNIT / math.log(2.0)))


def step_of(code):
    return jnp.exp(code * (math.log(2.0) / CODE_UNIT)) * (1.0 / LEVELS)


def column_peak(x):
    return jnp.max(jnp.abs(x), axis=0, keepdims=True)


def to_levels(x, code):
    return jnp.floor(x * (1.0 / step_of(code)) + 0.5).astype(jnp.int32).astype(jnp.int16)


def code_rows(codes):
    rest = jnp.zeros((16 - len(codes), codes[0].shape[1]), jnp.float32)
    return jnp.concatenate(codes + [rest], axis=0).astype(jnp.int32).astype(jnp.int16)


def wide_of(x):
    return x.astype(jnp.int32).astype(jnp.float32)


def compute_kernel(tiles, pos_groups, win, modes, grad_scale, me_ref, owner_ref, off_ref, *refs):
    packs = refs[:tiles]
    probe, amp, prop_re, prop_im, prop_t_re, prop_t_im, spot_ref = refs[tiles : tiles + 7]
    grads = refs[tiles + 7 : 2 * tiles + 7]
    away_ref, kept_ref = refs[2 * tiles + 7 : 2 * tiles + 9]
    (
        held, cat, wins, far, factor, right_a, right_b, left_a, left_b, obj_acc, probe_acc, gcat, outer_acc, gpack,
        in_sem, out_sem, piece_sem,
    ) = refs[2 * tiles + 9 :]
    half = win // 2
    quarter = win // 4
    me = me_ref[0]
    fetches = [pltpu.make_async_copy(packs[k], held.at[k], in_sem.at[k]) for k in range(tiles)]
    for fetch in fetches:
        fetch.start()

    for way in range(2):
        if way == 0:
            r_re, r_im = prop_t_re[...], prop_t_im[...]
            l_re, l_im = prop_re[...], prop_im[...]
        else:
            r_re, r_im = prop_re[...], -prop_im[...]
            l_re, l_im = prop_t_re[...], -prop_t_im[...]
        (rr, rr_low), (ri, ri_low) = halves(r_re), halves(r_im)
        for row, (a, b) in enumerate([(rr, ri), (rr, ri), (-ri, rr), (-ri, rr)]):
            right_a[way, row * win : (row + 1) * win, 0:win] = a
            right_a[way, row * win : (row + 1) * win, win : 2 * win] = b
        for row, (a, b) in enumerate([(rr_low, ri_low), (-ri_low, rr_low)]):
            right_b[way, row * win : (row + 1) * win, 0:win] = a
            right_b[way, row * win : (row + 1) * win, win : 2 * win] = b
        (lr, lr_low), (li, li_low) = halves(l_re), halves(l_im)
        for col, (a, b) in enumerate([(lr, li), (lr, li), (-li, lr), (-li, lr)]):
            left_a[way, 0:win, col * win : (col + 1) * win] = a
            left_a[way, win : 2 * win, col * win : (col + 1) * win] = b
        for col, (a, b) in enumerate([(lr_low, li_low), (-li_low, lr_low)]):
            left_b[way, 0:win, col * win : (col + 1) * win] = a
            left_b[way, win : 2 * win, col * win : (col + 1) * win] = b

    y_up, x_up, x_low, first = geometry(off_ref[0, 0], off_ref[0, 1], off_ref[1, 0], off_ref[1, 1])
    right = x_low > x_up
    strip = y_up // win
    rem = y_up - strip * win
    low_rem = lax.rem(rem, half)
    mid_block = (y_up + half) // half

    def slot_of(s):
        return lax.rem(me - owner_ref[jnp.minimum(s, tiles - 1)] + tiles, tiles)

    for fetch in fetches:
        fetch.wait()
    slots = [slot_of(strip + d) for d in range(3)]
    for part in range(2):
        for d in range(3):
            cat[part, d * win : (d + 1) * win, :] = held[slots[d], part, 0:win, :].astype(jnp.float32)
        for d in range(2):
            slot = slot_of((mid_block + d) // 2)
            for chunk in range(2):
                outer_acc[part, d * half + chunk * quarter : d * half + (chunk + 1) * quarter, :] = held[
                    slot, part, win : win + quarter, half * chunk : half * (chunk + 1)
                ].astype(jnp.float32)
    for part in range(2):
        upper = rows_from(cat, part, rem, win)
        wins[0, part] = upper
        wins[1, part, half:win, :] = rows_from(cat, part, rem + win, half)
        outer = rows_from(outer_acc, part, low_rem, half)
        wins[1, part, 0:half, 0:half] = jnp.where(right, upper[half:win, half:win], outer)
        wins[1, part, 0:half, half:win] = jnp.where(right, outer, upper[half:win, 0:half])

    def both(way, re, im):
        (re_h, re_l), (im_h, im_l) = halves(re), halves(im)
        mid = dot(jnp.concatenate([re_h, re_l, im_h, im_l], axis=1), right_a[way]) + dot(
            jnp.concatenate([re_h, im_h], axis=1), right_b[way]
        )
        (re_h, re_l), (im_h, im_l) = halves(mid[:, 0:win]), halves(mid[:, win : 2 * win])
        return dot(left_a[way], jnp.concatenate([re_h, re_l, im_h, im_l], axis=0)) + dot(
            left_b[way], jnp.concatenate([re_h, im_h], axis=0)
        )

    def forward(n, carry):
        q = n // modes
        m = lax.rem(n, modes)
        p_re, p_im = probe[m, 0], probe[m, 1]
        w_re, w_im = wins[q, 0], wins[q, 1]
        far[n] = both(0, p_re * w_re - p_im * w_im, p_re * w_im + p_im * w_re)
        return carry

    lax.fori_loop(0, 2 * modes, forward, 0)
    for q in range(2):
        total = jnp.zeros((win, win), jnp.float32)
        for m in range(modes):
            f_re, f_im = far[q * modes + m, 0:win, :], far[q * modes + m, win : 2 * win, :]
            total = total + (f_re * f_re + f_im * f_im)
        frame = jnp.where(first, q, 1 - q)
        measured = amp[frame].astype(jnp.float32)
        factor[q] = (1.0 - measured / jnp.maximum(jnp.sqrt(total), 1.0)) * grad_scale
    obj_acc[...] = jnp.zeros_like(obj_acc)
    probe_acc[...] = jnp.zeros_like(probe_acc)

    def backward(n, carry):
        q = n // modes
        m = lax.rem(n, modes)
        scale = factor[q]
        back = both(1, far[n, 0:win, :] * scale, far[n, win : 2 * win, :] * scale)
        b_re, b_im = back[0:win, :], back[win : 2 * win, :]
        p_re, p_im = probe[m, 0], probe[m, 1]
        w_re, w_im = wins[q, 0], wins[q, 1]
        obj_acc[q, 0] = obj_acc[q, 0] + (p_re * b_re + p_im * b_im)
        obj_acc[q, 1] = obj_acc[q, 1] + (p_re * b_im - p_im * b_re)
        probe_acc[m, 0] = probe_acc[m, 0] + (w_re * b_re + w_im * b_im)
        probe_acc[m, 1] = probe_acc[m, 1] + (w_re * b_im - w_im * b_re)
        return carry

    lax.fori_loop(0, 2 * modes, backward, 0)
    share = win // pos_groups
    spot = spot_ref[0]
    piece_copies = []
    for j in range(pos_groups):
        start = pl.multiple_of(jnp.bitwise_xor(spot, j) * share, share)
        home = (away_ref if j % 2 else kept_ref).at[j // 2]
        piece_copies.append(
            pltpu.make_async_copy(probe_acc.at[:, :, pl.ds(start, share), :], home, piece_sem.at[j])
        )
        piece_copies[-1].start()

    gcat[...] = jnp.zeros_like(gcat)
    outer_acc[...] = jnp.zeros_like(outer_acc)
    for part in range(2):
        low_a = obj_acc[1, part, 0:half, 0:half]
        low_b = obj_acc[1, part, 0:half, half:win]
        zero = jnp.zeros_like(low_a)
        obj_acc[0, part, half:win, 0:half] += jnp.where(right, zero, low_b)
        obj_acc[0, part, half:win, half:win] += jnp.where(right, low_a, zero)
        rows_to(gcat, part, rem, [obj_acc[0, part], obj_acc[1, part, half:win, :]])
        rows_to(outer_acc, part, low_rem, [jnp.where(right, low_b, low_a)])
        outer = outer_acc[part, 0:half, :] + outer_acc[part, half:win, :]
        outer_code = code_of(column_peak(outer))
        outer_levels = to_levels(outer, outer_code)
        for d in range(3):
            codes = []
            for level in range(2):
                rows = gcat[part, d * win + level * half : d * win + (level + 1) * half, :]
                codes.append(code_of(column_peak(rows)))
                gpack[d, part, level * half : (level + 1) * half, :] = to_levels(rows, codes[-1])
            for chunk in range(2):
                gpack[d, part, win : win + quarter, half * chunk : half * (chunk + 1)] = outer_levels[
                    chunk * quarter : (chunk + 1) * quarter, :
                ]
            codes.append(jnp.concatenate([outer_code, outer_code], axis=1))
            gpack[d, part, win + quarter : win + quarter + 16, :] = code_rows(codes)
    grad_copies = []
    for k in range(tiles):
        there = strip_held(owner_ref, lax.rem(me + k, tiles), tiles)
        d = jnp.clip(there - strip, 0, 2)
        grad_copies.append(pltpu.make_async_copy(gpack.at[d], grads[k], out_sem.at[k]))
        grad_copies[-1].start()
    for copy in piece_copies + grad_copies:
        copy.wait()


def propagate_call(tiles, pos_groups, win, modes, grad_scale):
    half = win // 2
    share = win // pos_groups
    pack_shape = (2, win + win // 4, win)
    grad_shape = (2, win + win // 4 + 16, win)
    smem = pl.BlockSpec(memory_space=pltpu.SMEM)
    vmem = pl.BlockSpec(memory_space=pltpu.VMEM)
    anywhere = pl.BlockSpec(memory_space=pl.ANY)
    return pl.pallas_call(
        functools.partial(compute_kernel, tiles, pos_groups, win, modes, grad_scale),
        out_shape=[jax.ShapeDtypeStruct(grad_shape, jnp.int16)] * tiles
        + [jax.ShapeDtypeStruct((pos_groups // 2, modes, 2, share, win), jnp.float32)] * 2,
        in_specs=[smem] * 3 + [anywhere] * tiles + [vmem] * 6 + [smem],
        out_specs=[anywhere] * (tiles + 2),
        scratch_shapes=[
            pltpu.VMEM((tiles,) + pack_shape, jnp.bfloat16),
            pltpu.VMEM((2, 3 * win, win), jnp.float32),
            pltpu.VMEM((2, 2, win, win), jnp.float32),
            pltpu.VMEM((2 * modes, 2 * win, win), jnp.float32),
            pltpu.VMEM((2, win, win), jnp.float32),
            pltpu.VMEM((2, 4 * win, 2 * win), jnp.bfloat16),
            pltpu.VMEM((2, 2 * win, 2 * win), jnp.bfloat16),
            pltpu.VMEM((2, 2 * win, 4 * win), jnp.bfloat16),
            pltpu.VMEM((2, 2 * win, 2 * win), jnp.bfloat16),
            pltpu.VMEM((2, 2, win, win), jnp.float32),
            pltpu.VMEM((modes, 2, win, win), jnp.float32),
            pltpu.VMEM((2, 3 * win, win), jnp.float32),
            pltpu.VMEM((2, win, half), jnp.float32),
            pltpu.VMEM((3,) + grad_shape, jnp.int16),
            pltpu.SemaphoreType.DMA((tiles,)),
            pltpu.SemaphoreType.DMA((tiles,)),
            pltpu.SemaphoreType.DMA((pos_groups,)),
        ],
        name="propagate",
    )


def probe_pack_kernel(blocks, rows, kept_ref, came_ref, total_ref, pack_ref):
    codes = []
    for b in range(blocks):
        total = kept_ref[b] + came_ref[b]
        total_ref[b] = total
        codes.append(code_of(column_peak(total)))
        pack_ref[b * rows : (b + 1) * rows, :] = to_levels(total, codes[-1])
    pack_ref[blocks * rows : blocks * rows + 16, :] = code_rows(codes)


def probe_sum_kernel(blocks, rows, own_ref, *refs):
    packs, total_ref = refs[:-1], refs[-1]
    scales = [step_of(wide_of(pack[blocks * rows : blocks * rows + 16, :])) for pack in packs]
    for b in range(blocks):
        total = own_ref[b]
        for pack, scale in zip(packs, scales):
            total = total + wide_of(pack[b * rows : (b + 1) * rows, :]) * scale[b : b + 1, :]
        total_ref[b] = total


def place_kernel(tiles, spots, steps_back, first, win, slab, me_ref, spot_ref, owner_ref, *refs):
    picks = [(j, k) for k in steps_back for j in range(spots)]
    count = len(picks)
    offs, refs = refs[:spots], refs[spots:]
    packs, refs = refs[:count], refs[count:]
    if not first:
        before, refs = refs[0], refs[1:]
    out_ref, held, acc, params, in_sem, out_sem = refs
    half = win // 2
    quarter = win // 4
    me = me_ref[0]
    strip = strip_held(owner_ref, me, tiles)
    base = strip * win
    first_col = spot_ref[0] * slab
    margin = 2 * win
    span = 3 * half
    if not first:
        resume = pltpu.make_async_copy(before, acc.at[:, :, margin : margin + slab], out_sem)
        resume.start()
    for n, (j, k) in enumerate(picks):
        off = offs[j]
        y_up, x_up, x_low, _ = geometry(off[2 * k, 0], off[2 * k, 1], off[2 * k + 1, 0], off[2 * k + 1, 1])
        left = jnp.minimum(x_up, x_low)
        hit = (y_up < base + win) & (y_up + span > base) & (left < first_col + slab) & (left + span > first_col)
        params[n, 0] = hit.astype(jnp.int32)
        params[n, 1] = y_up
        params[n, 2] = (x_low > x_up).astype(jnp.int32)
        params[n, 3] = left - first_col + margin

        @pl.when(hit)
        def _():
            pltpu.make_async_copy(packs[n], held.at[n], in_sem.at[n]).start()

    def clear(i, carry):
        acc[:, pl.ds(pl.multiple_of(i * 8, 8), 8), :] = jnp.zeros((2, 8, acc.shape[2]), jnp.float32)
        return carry

    if first:
        lax.fori_loop(0, win // 8, clear, 0)
    else:
        resume.wait()

    def one(n, carry):
        @pl.when(params[n, 0] == 1)
        def _():
            pltpu.make_async_copy(packs[0], held.at[n], in_sem.at[n]).wait()
            y_up = params[n, 1]
            right = params[n, 2]
            col = params[n, 3]
            start = pl.multiple_of((col // 128) * 128, 128)
            rem = col - start
            lanes = lane_iota((quarter, half))
            stay = lanes >= rem

            for part in range(2):
                steps = step_of(wide_of(held[n, part, win + quarter : win + quarter + 16, :]))
                for chunk in range(4):
                    row0 = chunk * quarter
                    level = chunk // 2
                    rows = base + row0 + row_iota((quarter, half))
                    low_first = (rows < y_up + win).astype(jnp.int32) == right
                    in_outer = (rows >= y_up + half) & (rows < y_up + win)
                    main = wide_of(held[n, part, row0 : row0 + quarter, :]) * steps[level : level + 1, :]
                    m0 = main[:, 0:half]
                    m1 = main[:, half:win]
                    side = held[n, part, win : win + quarter, half * (chunk % 2) : half * (chunk % 2 + 1)]
                    side = jnp.where(in_outer, wide_of(side) * steps[2:3, 0:half], 0.0)
                    cols = [
                        jnp.where(low_first, m0, jnp.where(right == 0, side, 0.0)),
                        jnp.where(low_first, m1, m0),
                        jnp.where(low_first, jnp.where(right == 1, side, 0.0), m1),
                    ]
                    spun = [pltpu.roll(c, rem, 1) for c in cols]
                    zero = jnp.zeros_like(m0)
                    shifted = [
                        jnp.where(stay, spun[0], zero),
                        jnp.where(stay, spun[1], spun[0]),
                        jnp.where(stay, spun[2], spun[1]),
                        jnp.where(stay, zero, spun[2]),
                    ]
                    for b in range(4):
                        at = pl.ds(pl.multiple_of(start + b * half, 128), half)
                        acc[part, row0 : row0 + quarter, at] += shifted[b]

        return carry

    lax.fori_loop(0, count, one, 0)
    out = pltpu.make_async_copy(acc.at[:, :, margin : margin + slab], out_ref, out_sem)
    out.start()
    out.wait()


def shifted(x, axis, count, k):
    return lax.ppermute(x, axis, [(i, (i + k) % count) for i in range(count)])


def swapped(x, axis, count, bit):
    return lax.ppermute(x, axis, [(i, i ^ bit) for i in range(count)])


def per_device_packed(object_field, probe, amplitude, offsets, strip_owner, chirp):
    tiles = lax.axis_size("tile")
    pos_groups = lax.axis_size("pos")
    pos_count, win, _ = amplitude.shape
    modes = probe.shape[0]
    width = object_field.shape[2]
    slab = width // pos_groups
    quarter = win // 4
    grad_scale = 1.0 / math.sqrt(pos_count * tiles * pos_groups)
    me = lax.axis_index("tile").astype(jnp.int32).reshape(1)
    spot = lax.axis_index("pos").astype(jnp.int32).reshape(1)
    smem = pl.BlockSpec(memory_space=pltpu.SMEM)
    vmem = pl.BlockSpec(memory_space=pltpu.VMEM)
    anywhere = pl.BlockSpec(memory_space=pl.ANY)
    pack_shape = (2, win + quarter, win)
    grad_shape = (2, win + quarter + 16, win)
    share = win // pos_groups

    offs = [offsets] + [shifted(offsets, "tile", tiles, tiles - k) for k in range(1, tiles)]

    def pack_for(asking, field):
        asked = len(asking)
        return pl.pallas_call(
            functools.partial(pack_kernel, tiles, asked, win, width),
            out_shape=[jax.ShapeDtypeStruct(pack_shape, jnp.bfloat16)] * asked,
            in_specs=[smem] * (2 + asked) + [anywhere],
            out_specs=[anywhere] * asked,
            scratch_shapes=[
                pltpu.VMEM((asked, 2, win, 2 * win), jnp.bfloat16),
                pltpu.VMEM((asked,) + pack_shape, jnp.bfloat16),
                pltpu.SMEM((asked, 4), jnp.int32),
                pltpu.SemaphoreType.DMA((asked,)),
                pltpu.SemaphoreType.DMA((asked,)),
            ],
            name="pack",
        )(me, strip_owner, *asking, field)

    packs = pack_for(offs[1:], object_field)
    packs, chirp, own_off = lax.optimization_barrier((packs, chirp, offsets))
    packs = pack_for([own_off], object_field) + packs
    column_offs = [jnp.concatenate([own_off] + [offs[tiles - k] for k in range(1, tiles)], axis=0)]
    bit = pos_groups // 2
    while bit:
        column_offs = column_offs + [swapped(o, "pos", pos_groups, bit) for o in column_offs]
        bit //= 2
    arrived = [packs[0]] + [shifted(packs[k], "tile", tiles, k) for k in range(1, tiles)]
    prop_re, prop_im = build_propagator(chirp)
    arrived, column_offs = lax.optimization_barrier((arrived, column_offs))
    results = propagate_call(tiles, pos_groups, win, modes, grad_scale)(
        me, strip_owner, offsets, *arrived, probe, amplitude, prop_re, prop_im, prop_re.T, prop_im.T, spot
    )
    grads, (away, kept) = results[:tiles], results[tiles:]

    column = [grads[0]] + [shifted(grads[k], "tile", tiles, k) for k in range(1, tiles)]
    columns = [column]
    bit = pos_groups // 2
    while bit:
        columns = columns + [[swapped(x, "pos", pos_groups, bit) for x in column] for column in columns]
        bit //= 2

    kept = kept + swapped(away, "pos", pos_groups, 1)
    bit = 2
    while kept.shape[0] > 2:
        kept = kept[0::2] + swapped(kept[1::2], "pos", pos_groups, bit)
        bit *= 2
    blocks = modes * 2
    came = swapped(kept[1], "pos", pos_groups, bit)
    probe_own, probe_pack = pl.pallas_call(
        functools.partial(probe_pack_kernel, blocks, share),
        out_shape=[
            jax.ShapeDtypeStruct((blocks, share, win), jnp.float32),
            jax.ShapeDtypeStruct((blocks * share + 16, win), jnp.int16),
        ],
        name="probe_pack",
    )(kept[0].reshape(blocks, share, win), came.reshape(blocks, share, win))
    probe_packs = [shifted(probe_pack, "tile", tiles, k) for k in range(1, tiles)]

    probe_out = pl.pallas_call(
        functools.partial(probe_sum_kernel, blocks, share),
        out_shape=jax.ShapeDtypeStruct((blocks, share, win), jnp.float32),
        name="probe_sum",
    )(probe_own, *probe_packs)

    spots = len(columns)
    placed = None
    near_first = near_to_far(tiles)
    for steps_back in ([0], near_first[:-1], near_first[-1:]):
        arrays = [columns[j][k] for k in steps_back for j in range(spots)]
        count = len(arrays)
        first = placed is None
        placed = pl.pallas_call(
            functools.partial(place_kernel, tiles, spots, steps_back, first, win, slab),
            out_shape=jax.ShapeDtypeStruct((2, win, slab), jnp.float32),
            in_specs=[smem] * (3 + spots) + [anywhere] * (count + (not first)),
            out_specs=anywhere,
            scratch_shapes=[
                pltpu.VMEM((count,) + grad_shape, jnp.int16),
                pltpu.VMEM((2, win, slab + 4 * win), jnp.float32),
                pltpu.SMEM((count, 4), jnp.int32),
                pltpu.SemaphoreType.DMA((count,)),
                pltpu.SemaphoreType.DMA,
            ],
        )(me, spot, strip_owner, *column_offs, *arrays, *([] if first else [placed]))
    return (placed, probe_out.reshape(modes, 2, share, win))


def per_device(object_field, probe, amplitude, offsets, strip_owner, chirp):
    pos_groups = lax.axis_size("pos")
    pos_count, win, _ = amplitude.shape
    width = object_field.shape[2]
    packed = (
        pos_count == 2
        and object_field.shape[1] == win
        and win == 256
        and pos_groups & (pos_groups - 1) == 0
        and width // pos_groups >= 2 * win
        and (width // pos_groups) % 128 == 0
        and pos_groups >= 4
        and (win // pos_groups) % 16 == 0
    )
    if not packed:
        return per_device_general(object_field, probe, amplitude, offsets, strip_owner, chirp)
    return per_device_packed(object_field, probe, amplitude, offsets, strip_owner, chirp)


def near_to_far(tiles):
    return sorted(range(1, tiles), key=lambda k: (min(k, tiles - k), k))


def solution(mesh):
    return jax.shard_map(
        per_device,
        mesh=mesh,
        in_specs=(
            P(None, ("groups", "tile"), None),
            P("groups", None, None, None),
            P(("groups", "tile", "pos"), None, None),
            P(("groups", "tile", "pos"), None),
            P("groups"),
            P(),
        ),
        out_specs=(P(None, ("groups", "tile"), "pos"), P("groups", None, "pos", None)),
        check_vma=False,
    )
```

```python
import functools
import math

import jax
import jax.numpy as jnp
from jax import lax
from jax.experimental import pallas as pl
from jax.experimental.pallas import tpu as pltpu
from jax.sharding import PartitionSpec as P


HIGHEST_PREC = lax.Precision.HIGHEST


def build_propagator(chirp):
    win_size = chirp.shape[0]
    freq_index = jnp.arange(win_size, dtype=jnp.int32)
    phase_grid = (
        2.0
        * math.pi
        / win_size
        * (freq_index[:, None] * freq_index[None, :] % win_size).astype(jnp.float32)
    )
    unit_norm = 1.0 / math.sqrt(win_size)
    fourier_re = jnp.cos(phase_grid) * unit_norm
    fourier_im = -jnp.sin(phase_grid) * unit_norm
    chirp_re = jnp.cos(chirp)[:, None]
    chirp_im = jnp.sin(chirp)[:, None]
    middle_re = chirp_re * fourier_re - chirp_im * fourier_im
    middle_im = chirp_re * fourier_im + chirp_im * fourier_re
    prop_re = jnp.dot(fourier_re, middle_re, precision=HIGHEST_PREC) + jnp.dot(
        fourier_im, middle_im, precision=HIGHEST_PREC
    )
    prop_im = jnp.dot(fourier_re, middle_im, precision=HIGHEST_PREC) - jnp.dot(
        fourier_im, middle_re, precision=HIGHEST_PREC
    )
    return (prop_re, prop_im)


def apply_both(left_re, left_im, part_re, part_im):
    first_re = jnp.einsum("ab,...bc->...ac", left_re, part_re, precision=HIGHEST_PREC) - jnp.einsum(
        "ab,...bc->...ac", left_im, part_im, precision=HIGHEST_PREC
    )
    first_im = jnp.einsum("ab,...bc->...ac", left_re, part_im, precision=HIGHEST_PREC) + jnp.einsum(
        "ab,...bc->...ac", left_im, part_re, precision=HIGHEST_PREC
    )
    out_re = jnp.einsum("...ab,cb->...ac", first_re, left_re, precision=HIGHEST_PREC) - jnp.einsum(
        "...ab,cb->...ac", first_im, left_im, precision=HIGHEST_PREC
    )
    out_im = jnp.einsum("...ab,cb->...ac", first_re, left_im, precision=HIGHEST_PREC) + jnp.einsum(
        "...ab,cb->...ac", first_im, left_re, precision=HIGHEST_PREC
    )
    return (out_re, out_im)


def position_terms(window, probe, amplitude, prop_re, prop_im, grad_scale):
    obj_re = window[:, None, 0]
    obj_im = window[:, None, 1]
    probe_re = probe[None, :, 0]
    probe_im = probe[None, :, 1]
    exit_re = probe_re * obj_re - probe_im * obj_im
    exit_im = probe_re * obj_im + probe_im * obj_re
    far_re, far_im = apply_both(prop_re, prop_im, exit_re, exit_im)
    intensity = jnp.sum(far_re * far_re + far_im * far_im, axis=1, keepdims=True)
    factor = (
        1.0 - amplitude[:, None].astype(jnp.float32) / jnp.maximum(jnp.sqrt(intensity), 1.0)
    ) * grad_scale
    back_re, back_im = apply_both(prop_re.T, -prop_im.T, far_re * factor, far_im * factor)
    obj_part_re = jnp.sum(probe_re * back_re + probe_im * back_im, axis=1)
    obj_part_im = jnp.sum(probe_re * back_im - probe_im * back_re, axis=1)
    probe_part_re = jnp.sum(obj_re * back_re + obj_im * back_im, axis=0)
    probe_part_im = jnp.sum(obj_re * back_im - obj_im * back_re, axis=0)
    return (
        jnp.stack([obj_part_re, obj_part_im], axis=1),
        jnp.stack([probe_part_re, probe_part_im], axis=1),
    )


def owner_of(strips, strip_owner):
    table = jnp.arange(strip_owner.shape[0], dtype=jnp.int32)
    return jnp.sum(jnp.where(strips[..., None] == table, strip_owner, 0), axis=-1)


def place_columns(strip_grad, start_cols, pieces):
    span_width = pieces.shape[-1]
    column_ids = start_cols[:, None] + jnp.arange(span_width, dtype=jnp.int32)[None, :]
    return strip_grad.at[:, :, column_ids].add(pieces.transpose(1, 2, 0, 3))


def per_device_general(object_field, probe, amplitude, offsets, strip_owner, chirp):
    tile_count = lax.axis_size("tile")
    pos_groups = lax.axis_size("pos")
    pos_count = amplitude.shape[0]
    win_size = probe.shape[-1]
    strip_rows = object_field.shape[1]
    width_all = object_field.shape[2]
    last_strip = tile_count - 1
    grad_scale = 1.0 / math.sqrt(pos_count * tile_count * pos_groups)
    prop_re, prop_im = build_propagator(chirp)
    everyone = lax.all_gather(offsets, "tile", axis=0, tiled=True)
    row_off = offsets[:, 0]
    strip_grad = jnp.zeros((2, strip_rows, width_all), jnp.float32)
    reach_strips = (win_size - 1) // strip_rows + 2
    flat_cols = everyone[:, 1]

    def cut_piece(start_col):
        return lax.dynamic_slice_in_dim(object_field, start_col, win_size, 2)

    pieces = jax.vmap(cut_piece)(flat_cols).reshape(tile_count, pos_count, 2, strip_rows, win_size)
    arrived = lax.all_to_all(pieces, "tile", split_axis=0, concat_axis=0, tiled=True)
    strip_of = row_off // strip_rows
    inside = row_off - strip_of * strip_rows
    strips = jnp.minimum(
        strip_of[:, None] + jnp.arange(reach_strips, dtype=jnp.int32)[None, :], last_strip
    )
    owners = owner_of(strips, strip_owner)
    slot_ids = jnp.arange(pos_count, dtype=jnp.int32)[:, None]
    stacked = (
        arrived[owners, slot_ids]
        .transpose(0, 2, 1, 3, 4)
        .reshape(pos_count, 2, reach_strips * strip_rows, win_size)
    )

    def cut_rows(stack_one, row_at):
        return lax.dynamic_slice_in_dim(stack_one, row_at, win_size, 1)

    windows = jax.vmap(cut_rows)(stacked, inside)
    obj_part, probe_sum = position_terms(
        windows.astype(jnp.float32), probe, amplitude, prop_re, prop_im, grad_scale
    )

    def put_rows(base_one, piece_one, row_at):
        return lax.dynamic_update_slice_in_dim(base_one, piece_one, row_at, 1)

    padded = jnp.zeros((pos_count, 2, reach_strips * strip_rows, win_size), jnp.float32)
    padded = jax.vmap(put_rows)(padded, obj_part, inside)
    split_grad = padded.reshape(pos_count, 2, reach_strips, strip_rows, win_size).transpose(
        0, 2, 1, 3, 4
    )
    outgoing = (
        jnp.zeros((tile_count, pos_count, 2, strip_rows, win_size), jnp.float32)
        .at[owners, slot_ids]
        .add(split_grad)
    )
    returned = lax.all_to_all(outgoing, "tile", split_axis=0, concat_axis=0, tiled=True)
    flat_back = returned.reshape(tile_count * pos_count, 2, strip_rows, win_size)
    strip_grad = place_columns(strip_grad, flat_cols, flat_back)
    strip_part = lax.psum_scatter(strip_grad, "pos", scatter_dimension=2, tiled=True)
    probe_total = lax.psum(probe_sum, ("tile", "pos"))
    row_share = win_size // pos_groups
    probe_out = lax.dynamic_slice_in_dim(
        probe_total, lax.axis_index("pos") * row_share, row_share, 2
    )
    return (strip_part, probe_out)


def grant(mib):
    return pltpu.CompilerParams(vmem_limit_bytes=mib << 20)


def strip_held(owner_ref, me, count):
    held = jnp.int32(0)
    for s in range(count):
        held = held + jnp.where(owner_ref[s] == me, s, 0).astype(jnp.int32)
    return held


def geometry(y_a, x_a, y_b, x_b):
    first = y_a < y_b
    return (
        jnp.where(first, y_a, y_b),
        jnp.where(first, x_a, x_b),
        jnp.where(first, x_b, x_a),
        first,
    )


def lane_iota(shape):
    return lax.broadcasted_iota(jnp.int32, shape, 1)


def row_iota(shape):
    return lax.broadcasted_iota(jnp.int32, shape, 0)


def pack_kernel(tiles, asked, win, width, me_ref, owner_ref, *refs):
    offs = refs[:asked]
    obj_ref = refs[asked]
    outs = refs[asked + 1 : 2 * asked + 1]
    buf, pack, params, in_sem, out_sem = refs[2 * asked + 1 :]
    half = win // 2
    quarter = win // 4
    strip = strip_held(owner_ref, me_ref[0], tiles)

    def fetch(k):
        start = pl.multiple_of(params[k, 3], 128)
        return pltpu.make_async_copy(
            obj_ref.at[:, :, pl.ds(start, 2 * win)], buf.at[k], in_sem.at[k]
        )

    for k in range(asked):
        y_up, x_up, x_low, _ = geometry(offs[k][0, 0], offs[k][0, 1], offs[k][1, 0], offs[k][1, 1])
        left = jnp.minimum(x_up, x_low)
        params[k, 0] = y_up
        params[k, 1] = (x_low > x_up).astype(jnp.int32)
        params[k, 3] = jnp.minimum((left // 128) * 128, width - 2 * win)
        params[k, 2] = left - params[k, 3]
        fetch(k).start()

    def one(k, carry):
        fetch(k).wait()
        y_up = params[k, 0]
        right = params[k, 1]
        rem = params[k, 2]
        turn = lax.rem(half - rem, half)
        keep = lane_iota((quarter, half)) < half - rem
        base = strip * win
        for part in range(2):
            for chunk in range(2):
                outer = []
                for level in range(2):
                    row0 = level * half + chunk * quarter
                    wide = buf[k, part, row0 : row0 + quarter, :].astype(jnp.float32)
                    spun = [
                        pltpu.roll(wide[:, half * b : half * (b + 1)], turn, 1) for b in range(4)
                    ]
                    cols = [jnp.where(keep, spun[b], spun[b + 1]) for b in range(3)]
                    rows = base + row0 + row_iota((quarter, half))
                    in_upper = (rows < y_up + win).astype(jnp.int32)
                    low_first = in_upper == right
                    pack[k, part, row0 : row0 + quarter, 0:half] = jnp.where(
                        low_first, cols[0], cols[1]
                    ).astype(pack.dtype)
                    pack[k, part, row0 : row0 + quarter, half:win] = jnp.where(
                        low_first, cols[1], cols[2]
                    ).astype(pack.dtype)
                    outer.append(jnp.where(right == 1, cols[2], cols[0]))
                high = base + half + chunk * quarter + row_iota((quarter, half))
                use_high = (high >= y_up + half) & (high < y_up + win)
                pack[k, part, win : win + quarter, half * chunk : half * (chunk + 1)] = jnp.where(
                    use_high, outer[1], outer[0]
                ).astype(pack.dtype)
        return carry

    for k in range(asked):
        one(k, 0)
        pltpu.make_async_copy(pack.at[k], outs[k], out_sem.at[k]).start()
    for k in range(asked):
        pltpu.make_async_copy(pack.at[k], outs[k], out_sem.at[k]).wait()


def halves(x):
    high = x.astype(jnp.bfloat16)
    return high, (x - high.astype(jnp.float32)).astype(jnp.bfloat16)


def dot(a, b):
    return lax.dot_general(a, b, (((1,), (0,)), ((), ())), preferred_element_type=jnp.float32)


def rows_from(ref, part, start, count):
    down = pl.multiple_of((start // 8) * 8, 8)
    rows = ref[part, pl.ds(down, count + 8), :]
    return pltpu.roll(rows, lax.rem(count + 8 - (start - down), count + 8), 0)[0:count]


def rows_to(ref, part, start, blocks):
    down = pl.multiple_of((start // 8) * 8, 8)
    rows = jnp.concatenate(blocks + [jnp.zeros((8, blocks[0].shape[1]), jnp.float32)], axis=0)
    ref[part, pl.ds(down, rows.shape[0]), :] = pltpu.roll(rows, start - down, 0)


LEVELS = 32600.0
CODE_UNIT = 256.0


def code_of(peak):
    return jnp.ceil(jnp.log(jnp.maximum(peak, 1e-30)) * (CODE_UNIT / math.log(2.0)))


def step_of(code):
    return jnp.exp(code * (math.log(2.0) / CODE_UNIT)) * (1.0 / LEVELS)


def column_peak(x):
    return jnp.max(jnp.abs(x), axis=0, keepdims=True)


def to_levels(x, code):
    return jnp.floor(x * (1.0 / step_of(code)) + 0.5).astype(jnp.int32).astype(jnp.int16)


def code_rows(codes):
    rest = jnp.zeros((16 - len(codes), codes[0].shape[1]), jnp.float32)
    return jnp.concatenate(codes + [rest], axis=0).astype(jnp.int32).astype(jnp.int16)


def wide_of(x):
    return x.astype(jnp.int32).astype(jnp.float32)


def compute_kernel(tiles, pos_groups, win, modes, grad_scale, me_ref, owner_ref, off_ref, *refs):
    packs = refs[:tiles]
    probe, amp, prop_re, prop_im, prop_t_re, prop_t_im, spot_ref = refs[tiles : tiles + 7]
    grads = refs[tiles + 7 : 2 * tiles + 7]
    away_ref, kept_ref = refs[2 * tiles + 7 : 2 * tiles + 9]
    (
        held, cat, wins, far, factor, right_m, left_m, obj_acc, probe_acc, gcat, outer_acc, gpack,
        in_sem, out_sem, piece_sem,
    ) = refs[2 * tiles + 9 :]
    half = win // 2
    quarter = win // 4
    me = me_ref[0]
    fetches = [pltpu.make_async_copy(packs[k], held.at[k], in_sem.at[k]) for k in range(tiles)]
    for fetch in fetches:
        fetch.start()

    for way in range(2):
        if way == 0:
            right, left = (prop_t_re[...], prop_t_im[...]), (prop_re[...], prop_im[...])
        else:
            right, left = (prop_re[...], -prop_im[...]), (prop_t_re[...], -prop_t_im[...])
        for at, (r, l) in enumerate(zip(right + (right[0] + right[1],), left + (left[0] + left[1],))):
            r_h, r_l = halves(r)
            l_h, l_l = halves(l)
            for third, (rr, ll) in enumerate([(r_h, l_h), (r_h, l_h), (r_l, l_l)]):
                right_m[way, at, third * win : (third + 1) * win, :] = rr
                left_m[way, at, :, third * win : (third + 1) * win] = ll

    y_up, x_up, x_low, first = geometry(off_ref[0, 0], off_ref[0, 1], off_ref[1, 0], off_ref[1, 1])
    right = x_low > x_up
    strip = y_up // win
    rem = y_up - strip * win
    low_rem = lax.rem(rem, half)
    mid_block = (y_up + half) // half

    def slot_of(s):
        return lax.rem(me - owner_ref[jnp.minimum(s, tiles - 1)] + tiles, tiles)

    for fetch in fetches:
        fetch.wait()
    slots = [slot_of(strip + d) for d in range(3)]
    for part in range(2):
        for d in range(3):
            cat[part, d * win : (d + 1) * win, :] = held[slots[d], part, 0:win, :].astype(jnp.float32)
        for d in range(2):
            slot = slot_of((mid_block + d) // 2)
            for chunk in range(2):
                outer_acc[part, d * half + chunk * quarter : d * half + (chunk + 1) * quarter, :] = held[
                    slot, part, win : win + quarter, half * chunk : half * (chunk + 1)
                ].astype(jnp.float32)
    for part in range(2):
        upper = rows_from(cat, part, rem, win)
        wins[0, part] = upper
        wins[1, part, half:win, :] = rows_from(cat, part, rem + win, half)
        outer = rows_from(outer_acc, part, low_rem, half)
        wins[1, part, 0:half, 0:half] = jnp.where(right, upper[half:win, half:win], outer)
        wins[1, part, 0:half, half:win] = jnp.where(right, outer, upper[half:win, 0:half])

    def three(re, im, side):
        both_re, both_im, both_sum = side(re, 0), side(im, 1), side(re + im, 2)
        return both_re - both_im, both_sum - both_re - both_im

    def both(way, re, im):
        def from_right(x, at):
            high, low = halves(x)
            return dot(jnp.concatenate([high, low, high], axis=1), right_m[way, at])

        def from_left(x, at):
            high, low = halves(x)
            return dot(left_m[way, at], jnp.concatenate([high, low, high], axis=0))

        return three(*three(re, im, from_right), from_left)

    def forward(n, carry):
        q = n // modes
        m = lax.rem(n, modes)
        p_re, p_im = probe[m, 0], probe[m, 1]
        w_re, w_im = wins[q, 0], wins[q, 1]
        far[n, 0:win, :], far[n, win : 2 * win, :] = both(0, p_re * w_re - p_im * w_im, p_re * w_im + p_im * w_re)
        return carry

    lax.fori_loop(0, 2 * modes, forward, 0, unroll=2)
    for q in range(2):
        total = jnp.zeros((win, win), jnp.float32)
        for m in range(modes):
            f_re, f_im = far[q * modes + m, 0:win, :], far[q * modes + m, win : 2 * win, :]
            total = total + (f_re * f_re + f_im * f_im)
        frame = jnp.where(first, q, 1 - q)
        measured = amp[frame]
        factor[q] = (1.0 - measured * lax.rsqrt(jnp.maximum(total, 1.0))) * grad_scale
    obj_acc[...] = jnp.zeros_like(obj_acc)
    probe_acc[...] = jnp.zeros_like(probe_acc)

    def backward(n, carry):
        q = n // modes
        m = lax.rem(n, modes)
        scale = factor[q]
        b_re, b_im = both(1, far[n, 0:win, :] * scale, far[n, win : 2 * win, :] * scale)
        p_re, p_im = probe[m, 0], probe[m, 1]
        w_re, w_im = wins[q, 0], wins[q, 1]
        obj_acc[q, 0] = obj_acc[q, 0] + (p_re * b_re + p_im * b_im)
        obj_acc[q, 1] = obj_acc[q, 1] + (p_re * b_im - p_im * b_re)
        probe_acc[m, 0] = probe_acc[m, 0] + (w_re * b_re + w_im * b_im)
        probe_acc[m, 1] = probe_acc[m, 1] + (w_re * b_im - w_im * b_re)
        return carry

    lax.fori_loop(0, 2 * modes, backward, 0, unroll=2)
    share = win // pos_groups
    spot = spot_ref[0]
    piece_copies = []
    for j in range(pos_groups):
        start = pl.multiple_of(jnp.bitwise_xor(spot, j) * share, share)
        home = (away_ref if j % 2 else kept_ref).at[j // 2]
        piece_copies.append(
            pltpu.make_async_copy(probe_acc.at[:, :, pl.ds(start, share), :], home, piece_sem.at[j])
        )
        piece_copies[-1].start()

    gcat[...] = jnp.zeros_like(gcat)
    outer_acc[...] = jnp.zeros_like(outer_acc)
    for part in range(2):
        low_a = obj_acc[1, part, 0:half, 0:half]
        low_b = obj_acc[1, part, 0:half, half:win]
        zero = jnp.zeros_like(low_a)
        obj_acc[0, part, half:win, 0:half] += jnp.where(right, zero, low_b)
        obj_acc[0, part, half:win, half:win] += jnp.where(right, low_a, zero)
        rows_to(gcat, part, rem, [obj_acc[0, part], obj_acc[1, part, half:win, :]])
        rows_to(outer_acc, part, low_rem, [jnp.where(right, low_b, low_a)])
        outer = outer_acc[part, 0:half, :] + outer_acc[part, half:win, :]
        outer_code = code_of(column_peak(outer))
        outer_levels = to_levels(outer, outer_code)
        for d in range(3):
            codes = []
            for level in range(2):
                rows = gcat[part, d * win + level * half : d * win + (level + 1) * half, :]
                codes.append(code_of(column_peak(rows)))
                gpack[d, part, level * half : (level + 1) * half, :] = to_levels(rows, codes[-1])
            for chunk in range(2):
                gpack[d, part, win : win + quarter, half * chunk : half * (chunk + 1)] = outer_levels[
                    chunk * quarter : (chunk + 1) * quarter, :
                ]
            codes.append(jnp.concatenate([outer_code, outer_code], axis=1))
            gpack[d, part, win + quarter : win + quarter + 16, :] = code_rows(codes)
    grad_copies = []
    for k in range(tiles):
        there = strip_held(owner_ref, lax.rem(me + k, tiles), tiles)
        d = jnp.clip(there - strip, 0, 2)
        grad_copies.append(pltpu.make_async_copy(gpack.at[d], grads[k], out_sem.at[k]))
        grad_copies[-1].start()
    for copy in piece_copies + grad_copies:
        copy.wait()


def propagate_call(tiles, pos_groups, win, modes, grad_scale):
    half = win // 2
    share = win // pos_groups
    pack_shape = (2, win + win // 4, win)
    grad_shape = (2, win + win // 4 + 16, win)
    smem = pl.BlockSpec(memory_space=pltpu.SMEM)
    vmem = pl.BlockSpec(memory_space=pltpu.VMEM)
    anywhere = pl.BlockSpec(memory_space=pl.ANY)
    return pl.pallas_call(
        functools.partial(compute_kernel, tiles, pos_groups, win, modes, grad_scale),
        out_shape=[jax.ShapeDtypeStruct(grad_shape, jnp.int16)] * tiles
        + [jax.ShapeDtypeStruct((pos_groups // 2, modes, 2, share, win), jnp.float32)] * 2,
        in_specs=[smem] * 3 + [anywhere] * tiles + [vmem] * 6 + [smem],
        out_specs=[anywhere] * (tiles + 2),
        scratch_shapes=[
            pltpu.VMEM((tiles,) + pack_shape, jnp.bfloat16),
            pltpu.VMEM((2, 3 * win, win), jnp.float32),
            pltpu.VMEM((2, 2, win, win), jnp.float32),
            pltpu.VMEM((2 * modes, 2 * win, win), jnp.float32),
            pltpu.VMEM((2, win, win), jnp.float32),
            pltpu.VMEM((2, 3, 3 * win, win), jnp.bfloat16),
            pltpu.VMEM((2, 3, win, 3 * win), jnp.bfloat16),
            pltpu.VMEM((2, 2, win, win), jnp.float32),
            pltpu.VMEM((modes, 2, win, win), jnp.float32),
            pltpu.VMEM((2, 3 * win, win), jnp.float32),
            pltpu.VMEM((2, win, half), jnp.float32),
            pltpu.VMEM((3,) + grad_shape, jnp.int16),
            pltpu.SemaphoreType.DMA((tiles,)),
            pltpu.SemaphoreType.DMA((tiles,)),
            pltpu.SemaphoreType.DMA((pos_groups,)),
        ],
        compiler_params=grant(40),
        name="propagate",
    )


def packed(total, pack_ref, b, rows):
    code = code_of(column_peak(total))
    pack_ref[b * rows : (b + 1) * rows, :] = to_levels(total, code)
    return code


def probe_cross_kernel(blocks, rows, kept_ref, came_ref, total_ref, pack_ref):
    codes = []
    for b in range(blocks):
        total_ref[b] = kept_ref[0, b] + came_ref[0, b]
        codes.append(packed(kept_ref[1, b] + came_ref[1, b], pack_ref, b, rows))
    pack_ref[blocks * rows : blocks * rows + 16, :] = code_rows(codes)


def probe_close_kernel(blocks, rows, kept_ref, came_ref, total_ref, pack_ref):
    scale = step_of(wide_of(came_ref[blocks * rows : blocks * rows + 16, :]))
    codes = []
    for b in range(blocks):
        total = kept_ref[b] + wide_of(came_ref[b * rows : (b + 1) * rows, :]) * scale[b : b + 1, :]
        total_ref[b] = total
        codes.append(packed(total, pack_ref, b, rows))
    pack_ref[blocks * rows : blocks * rows + 16, :] = code_rows(codes)


def probe_sum_kernel(blocks, rows, own_ref, *refs):
    packs, total_ref = refs[:-1], refs[-1]
    scales = [step_of(wide_of(pack[blocks * rows : blocks * rows + 16, :])) for pack in packs]
    for b in range(blocks):
        total = own_ref[b]
        for pack, scale in zip(packs, scales):
            total = total + wide_of(pack[b * rows : (b + 1) * rows, :]) * scale[b : b + 1, :]
        total_ref[b] = total


def place_kernel(tiles, spots, steps_back, first, win, slab, me_ref, spot_ref, owner_ref, *refs):
    picks = [(j, k) for k in steps_back for j in range(spots)]
    count = len(picks)
    offs, refs = refs[:spots], refs[spots:]
    packs, refs = refs[:count], refs[count:]
    if not first:
        before, refs = refs[0], refs[1:]
    out_ref, held, acc, params, in_sem, out_sem = refs
    half = win // 2
    quarter = win // 4
    me = me_ref[0]
    strip = strip_held(owner_ref, me, tiles)
    base = strip * win
    first_col = spot_ref[0] * slab
    margin = 2 * win
    span = 3 * half
    if not first:
        resume = pltpu.make_async_copy(before, acc.at[:, :, margin : margin + slab], out_sem)
        resume.start()
    for n, (j, k) in enumerate(picks):
        off = offs[j]
        y_up, x_up, x_low, _ = geometry(off[2 * k, 0], off[2 * k, 1], off[2 * k + 1, 0], off[2 * k + 1, 1])
        left = jnp.minimum(x_up, x_low)
        hit = (y_up < base + win) & (y_up + span > base) & (left < first_col + slab) & (left + span > first_col)
        params[n, 0] = hit.astype(jnp.int32)
        params[n, 1] = y_up
        params[n, 2] = (x_low > x_up).astype(jnp.int32)
        params[n, 3] = left - first_col + margin

        @pl.when(hit)
        def _():
            pltpu.make_async_copy(packs[n], held.at[n], in_sem.at[n]).start()

    def clear(i, carry):
        acc[:, pl.ds(pl.multiple_of(i * 8, 8), 8), :] = jnp.zeros((2, 8, acc.shape[2]), jnp.float32)
        return carry

    if first:
        lax.fori_loop(0, win // 8, clear, 0)
    else:
        resume.wait()

    def one(n, carry):
        @pl.when(params[n, 0] == 1)
        def _():
            pltpu.make_async_copy(packs[0], held.at[n], in_sem.at[n]).wait()
            y_up = params[n, 1]
            right = params[n, 2]
            col = params[n, 3]
            start = pl.multiple_of((col // 128) * 128, 128)
            rem = col - start
            lanes = lane_iota((quarter, half))
            stay = lanes >= rem

            def strip_piece(part, chunk, steps):
                row0 = chunk * quarter
                level = chunk // 2
                rows = base + row0 + row_iota((quarter, half))
                low_first = (rows < y_up + win).astype(jnp.int32) == right
                in_outer = (rows >= y_up + half) & (rows < y_up + win)
                main = wide_of(held[n, part, row0 : row0 + quarter, :]) * steps[level : level + 1, :]
                m0 = main[:, 0:half]
                m1 = main[:, half:win]
                side = held[n, part, win : win + quarter, half * (chunk % 2) : half * (chunk % 2 + 1)]
                side = jnp.where(in_outer, wide_of(side) * steps[2:3, 0:half], 0.0)
                cols = [
                    jnp.where(low_first, m0, jnp.where(right == 0, side, 0.0)),
                    jnp.where(low_first, m1, m0),
                    jnp.where(low_first, jnp.where(right == 1, side, 0.0), m1),
                ]
                spun = [pltpu.roll(c, rem, 1) for c in cols]
                zero = jnp.zeros_like(m0)
                moved = [
                    jnp.where(stay, spun[0], zero),
                    jnp.where(stay, spun[1], spun[0]),
                    jnp.where(stay, spun[2], spun[1]),
                    jnp.where(stay, zero, spun[2]),
                ]
                for b in range(4):
                    at = pl.ds(pl.multiple_of(start + b * half, 128), half)
                    acc[part, row0 : row0 + quarter, at] += moved[b]

            steps = [step_of(wide_of(held[n, part, win + quarter : win + quarter + 16, :])) for part in range(2)]
            for chunk in range(4):
                low = base + chunk * quarter

                @pl.when((low < y_up + span) & (low + quarter > y_up))
                def _():
                    for part in range(2):
                        strip_piece(part, chunk, steps[part])

        return carry

    lax.fori_loop(0, count, one, 0)
    out = pltpu.make_async_copy(acc.at[:, :, margin : margin + slab], out_ref, out_sem)
    out.start()
    out.wait()


def shifted(x, axis, count, k):
    return lax.ppermute(x, axis, [(i, (i + k) % count) for i in range(count)])


def swapped(x, axis, count, bit):
    return lax.ppermute(x, axis, [(i, i ^ bit) for i in range(count)])


def per_device_packed(object_field, probe, amplitude, offsets, strip_owner, chirp):
    tiles = lax.axis_size("tile")
    pos_groups = lax.axis_size("pos")
    pos_count, win, _ = amplitude.shape
    modes = probe.shape[0]
    width = object_field.shape[2]
    slab = width // pos_groups
    quarter = win // 4
    grad_scale = 1.0 / math.sqrt(pos_count * tiles * pos_groups)
    me = lax.axis_index("tile").astype(jnp.int32).reshape(1)
    spot = lax.axis_index("pos").astype(jnp.int32).reshape(1)
    smem = pl.BlockSpec(memory_space=pltpu.SMEM)
    vmem = pl.BlockSpec(memory_space=pltpu.VMEM)
    anywhere = pl.BlockSpec(memory_space=pl.ANY)
    pack_shape = (2, win + quarter, win)
    grad_shape = (2, win + quarter + 16, win)
    share = win // pos_groups

    offs = [offsets] + [shifted(offsets, "tile", tiles, tiles - k) for k in range(1, tiles)]

    def pack_for(asking, field):
        asked = len(asking)
        return pl.pallas_call(
            functools.partial(pack_kernel, tiles, asked, win, width),
            out_shape=[jax.ShapeDtypeStruct(pack_shape, jnp.bfloat16)] * asked,
            in_specs=[smem] * (2 + asked) + [anywhere],
            out_specs=[anywhere] * asked,
            scratch_shapes=[
                pltpu.VMEM((asked, 2, win, 2 * win), jnp.bfloat16),
                pltpu.VMEM((asked,) + pack_shape, jnp.bfloat16),
                pltpu.SMEM((asked, 4), jnp.int32),
                pltpu.SemaphoreType.DMA((asked,)),
                pltpu.SemaphoreType.DMA((asked,)),
            ],
            compiler_params=grant(60),
            name="pack",
        )(me, strip_owner, *asking, field)

    packs = pack_for(offs[1:], object_field)
    packs, chirp, own_off = lax.optimization_barrier((packs, chirp, offsets))
    packs = pack_for([own_off], object_field) + packs
    column_offs = [jnp.concatenate([own_off] + [offs[tiles - k] for k in range(1, tiles)], axis=0)]
    bit = pos_groups // 2
    while bit:
        column_offs = column_offs + [swapped(o, "pos", pos_groups, bit) for o in column_offs]
        bit //= 2
    arrived = [packs[0]] + [shifted(packs[k], "tile", tiles, k) for k in range(1, tiles)]
    prop_re, prop_im = build_propagator(chirp)
    measured = lax.optimization_barrier((amplitude, chirp))[0].astype(jnp.float32)
    arrived, column_offs = lax.optimization_barrier((arrived, column_offs))
    results = propagate_call(tiles, pos_groups, win, modes, grad_scale)(
        me, strip_owner, offsets, *arrived, probe, measured, prop_re, prop_im, prop_re.T, prop_im.T, spot
    )
    grads, (away, kept) = results[:tiles], results[tiles:]

    column = [grads[0]] + [shifted(grads[k], "tile", tiles, k) for k in range(1, tiles)]
    columns = [column]
    bit = pos_groups // 2
    while bit:
        columns = columns + [[swapped(x, "pos", pos_groups, bit) for x in column] for column in columns]
        bit //= 2

    blocks = modes * 2

    def probe_step(kernel, *parts):
        return pl.pallas_call(
            functools.partial(kernel, blocks, share),
            out_shape=[
                jax.ShapeDtypeStruct((blocks, share, win), jnp.float32),
                jax.ShapeDtypeStruct((blocks * share + 16, win), jnp.int16),
            ],
            compiler_params=grant(8),
        )(*parts)

    pair = (2, blocks, share, win)
    came = swapped(away, "pos", pos_groups, 1).reshape(pair)
    probe_own, probe_pack = probe_step(probe_cross_kernel, kept.reshape(pair), came)
    came = swapped(probe_pack, "pos", pos_groups, 2)
    probe_own, probe_pack = probe_step(probe_close_kernel, probe_own, came)
    probe_packs = [shifted(probe_pack, "tile", tiles, k) for k in range(1, tiles)]

    probe_out = pl.pallas_call(
        functools.partial(probe_sum_kernel, blocks, share),
        out_shape=jax.ShapeDtypeStruct((blocks, share, win), jnp.float32),
        compiler_params=grant(4),
        name="probe_sum",
    )(probe_own, *probe_packs)

    spots = len(columns)
    placed = None
    near_first = near_to_far(tiles)
    for steps_back in ([0], near_first[:-1], near_first[-1:]):
        arrays = [columns[j][k] for k in steps_back for j in range(spots)]
        count = len(arrays)
        first = placed is None
        placed = pl.pallas_call(
            functools.partial(place_kernel, tiles, spots, steps_back, first, win, slab),
            out_shape=jax.ShapeDtypeStruct((2, win, slab), jnp.float32),
            in_specs=[smem] * (3 + spots) + [anywhere] * (count + (not first)),
            out_specs=anywhere,
            scratch_shapes=[
                pltpu.VMEM((count,) + grad_shape, jnp.int16),
                pltpu.VMEM((2, win, slab + 4 * win), jnp.float32),
                pltpu.SMEM((count, 4), jnp.int32),
                pltpu.SemaphoreType.DMA((count,)),
                pltpu.SemaphoreType.DMA,
            ],
            compiler_params=grant(16),
        )(me, spot, strip_owner, *column_offs, *arrays, *([] if first else [placed]))
    return (placed, probe_out.reshape(modes, 2, share, win))


def per_device(object_field, probe, amplitude, offsets, strip_owner, chirp):
    pos_groups = lax.axis_size("pos")
    pos_count, win, _ = amplitude.shape
    width = object_field.shape[2]
    packed = (
        pos_count == 2
        and object_field.shape[1] == win
        and win == 256
        and width // pos_groups >= 2 * win
        and (width // pos_groups) % 128 == 0
        and pos_groups == 4
        and (win // pos_groups) % 16 == 0
    )
    if not packed:
        return per_device_general(object_field, probe, amplitude, offsets, strip_owner, chirp)
    return per_device_packed(object_field, probe, amplitude, offsets, strip_owner, chirp)


def near_to_far(tiles):
    return sorted(range(1, tiles), key=lambda k: (min(k, tiles - k), k))


def solution(mesh):
    return jax.shard_map(
        per_device,
        mesh=mesh,
        in_specs=(
            P(None, ("groups", "tile"), None),
            P("groups", None, None, None),
            P(("groups", "tile", "pos"), None, None),
            P(("groups", "tile", "pos"), None),
            P("groups"),
            P(),
        ),
        out_specs=(P(None, ("groups", "tile"), "pos"), P("groups", None, "pos", None)),
        check_vma=False,
    )
```

```python
import functools
import math

import jax
import jax.numpy as jnp
from jax import lax
from jax.experimental import pallas as pl
from jax.experimental.pallas import tpu as pltpu
from jax.sharding import PartitionSpec as P


HIGHEST_PREC = lax.Precision.HIGHEST


def build_propagator(chirp):
    win_size = chirp.shape[0]
    freq_index = jnp.arange(win_size, dtype=jnp.int32)
    phase_grid = (
        2.0
        * math.pi
        / win_size
        * (freq_index[:, None] * freq_index[None, :] % win_size).astype(jnp.float32)
    )
    unit_norm = 1.0 / math.sqrt(win_size)
    fourier_re = jnp.cos(phase_grid) * unit_norm
    fourier_im = -jnp.sin(phase_grid) * unit_norm
    chirp_re = jnp.cos(chirp)[:, None]
    chirp_im = jnp.sin(chirp)[:, None]
    middle_re = chirp_re * fourier_re - chirp_im * fourier_im
    middle_im = chirp_re * fourier_im + chirp_im * fourier_re
    prop_re = jnp.dot(fourier_re, middle_re, precision=HIGHEST_PREC) + jnp.dot(
        fourier_im, middle_im, precision=HIGHEST_PREC
    )
    prop_im = jnp.dot(fourier_re, middle_im, precision=HIGHEST_PREC) - jnp.dot(
        fourier_im, middle_re, precision=HIGHEST_PREC
    )
    return (prop_re, prop_im)


def apply_both(left_re, left_im, part_re, part_im):
    first_re = jnp.einsum("ab,...bc->...ac", left_re, part_re, precision=HIGHEST_PREC) - jnp.einsum(
        "ab,...bc->...ac", left_im, part_im, precision=HIGHEST_PREC
    )
    first_im = jnp.einsum("ab,...bc->...ac", left_re, part_im, precision=HIGHEST_PREC) + jnp.einsum(
        "ab,...bc->...ac", left_im, part_re, precision=HIGHEST_PREC
    )
    out_re = jnp.einsum("...ab,cb->...ac", first_re, left_re, precision=HIGHEST_PREC) - jnp.einsum(
        "...ab,cb->...ac", first_im, left_im, precision=HIGHEST_PREC
    )
    out_im = jnp.einsum("...ab,cb->...ac", first_re, left_im, precision=HIGHEST_PREC) + jnp.einsum(
        "...ab,cb->...ac", first_im, left_re, precision=HIGHEST_PREC
    )
    return (out_re, out_im)


def position_terms(window, probe, amplitude, prop_re, prop_im, grad_scale):
    obj_re = window[:, None, 0]
    obj_im = window[:, None, 1]
    probe_re = probe[None, :, 0]
    probe_im = probe[None, :, 1]
    exit_re = probe_re * obj_re - probe_im * obj_im
    exit_im = probe_re * obj_im + probe_im * obj_re
    far_re, far_im = apply_both(prop_re, prop_im, exit_re, exit_im)
    intensity = jnp.sum(far_re * far_re + far_im * far_im, axis=1, keepdims=True)
    factor = (
        1.0 - amplitude[:, None].astype(jnp.float32) / jnp.maximum(jnp.sqrt(intensity), 1.0)
    ) * grad_scale
    back_re, back_im = apply_both(prop_re.T, -prop_im.T, far_re * factor, far_im * factor)
    obj_part_re = jnp.sum(probe_re * back_re + probe_im * back_im, axis=1)
    obj_part_im = jnp.sum(probe_re * back_im - probe_im * back_re, axis=1)
    probe_part_re = jnp.sum(obj_re * back_re + obj_im * back_im, axis=0)
    probe_part_im = jnp.sum(obj_re * back_im - obj_im * back_re, axis=0)
    return (
        jnp.stack([obj_part_re, obj_part_im], axis=1),
        jnp.stack([probe_part_re, probe_part_im], axis=1),
    )


def owner_of(strips, strip_owner):
    table = jnp.arange(strip_owner.shape[0], dtype=jnp.int32)
    return jnp.sum(jnp.where(strips[..., None] == table, strip_owner, 0), axis=-1)


def place_columns(strip_grad, start_cols, pieces):
    span_width = pieces.shape[-1]
    column_ids = start_cols[:, None] + jnp.arange(span_width, dtype=jnp.int32)[None, :]
    return strip_grad.at[:, :, column_ids].add(pieces.transpose(1, 2, 0, 3))


def per_device_general(object_field, probe, amplitude, offsets, strip_owner, chirp):
    tile_count = lax.axis_size("tile")
    pos_groups = lax.axis_size("pos")
    pos_count = amplitude.shape[0]
    win_size = probe.shape[-1]
    strip_rows = object_field.shape[1]
    width_all = object_field.shape[2]
    last_strip = tile_count - 1
    grad_scale = 1.0 / math.sqrt(pos_count * tile_count * pos_groups)
    prop_re, prop_im = build_propagator(chirp)
    everyone = lax.all_gather(offsets, "tile", axis=0, tiled=True)
    row_off = offsets[:, 0]
    strip_grad = jnp.zeros((2, strip_rows, width_all), jnp.float32)
    reach_strips = (win_size - 1) // strip_rows + 2
    flat_cols = everyone[:, 1]

    def cut_piece(start_col):
        return lax.dynamic_slice_in_dim(object_field, start_col, win_size, 2)

    pieces = jax.vmap(cut_piece)(flat_cols).reshape(tile_count, pos_count, 2, strip_rows, win_size)
    arrived = lax.all_to_all(pieces, "tile", split_axis=0, concat_axis=0, tiled=True)
    strip_of = row_off // strip_rows
    inside = row_off - strip_of * strip_rows
    strips = jnp.minimum(
        strip_of[:, None] + jnp.arange(reach_strips, dtype=jnp.int32)[None, :], last_strip
    )
    owners = owner_of(strips, strip_owner)
    slot_ids = jnp.arange(pos_count, dtype=jnp.int32)[:, None]
    stacked = (
        arrived[owners, slot_ids]
        .transpose(0, 2, 1, 3, 4)
        .reshape(pos_count, 2, reach_strips * strip_rows, win_size)
    )

    def cut_rows(stack_one, row_at):
        return lax.dynamic_slice_in_dim(stack_one, row_at, win_size, 1)

    windows = jax.vmap(cut_rows)(stacked, inside)
    obj_part, probe_sum = position_terms(
        windows.astype(jnp.float32), probe, amplitude, prop_re, prop_im, grad_scale
    )

    def put_rows(base_one, piece_one, row_at):
        return lax.dynamic_update_slice_in_dim(base_one, piece_one, row_at, 1)

    padded = jnp.zeros((pos_count, 2, reach_strips * strip_rows, win_size), jnp.float32)
    padded = jax.vmap(put_rows)(padded, obj_part, inside)
    split_grad = padded.reshape(pos_count, 2, reach_strips, strip_rows, win_size).transpose(
        0, 2, 1, 3, 4
    )
    outgoing = (
        jnp.zeros((tile_count, pos_count, 2, strip_rows, win_size), jnp.float32)
        .at[owners, slot_ids]
        .add(split_grad)
    )
    returned = lax.all_to_all(outgoing, "tile", split_axis=0, concat_axis=0, tiled=True)
    flat_back = returned.reshape(tile_count * pos_count, 2, strip_rows, win_size)
    strip_grad = place_columns(strip_grad, flat_cols, flat_back)
    strip_part = lax.psum_scatter(strip_grad, "pos", scatter_dimension=2, tiled=True)
    probe_total = lax.psum(probe_sum, ("tile", "pos"))
    row_share = win_size // pos_groups
    probe_out = lax.dynamic_slice_in_dim(
        probe_total, lax.axis_index("pos") * row_share, row_share, 2
    )
    return (strip_part, probe_out)


def grant(mib):
    return pltpu.CompilerParams(vmem_limit_bytes=mib << 20)


def strip_held(owner_ref, me, count):
    held = jnp.int32(0)
    for s in range(count):
        held = held + jnp.where(owner_ref[s] == me, s, 0).astype(jnp.int32)
    return held


def geometry(y_a, x_a, y_b, x_b):
    first = y_a < y_b
    return (
        jnp.where(first, y_a, y_b),
        jnp.where(first, x_a, x_b),
        jnp.where(first, x_b, x_a),
        first,
    )


def lane_iota(shape):
    return lax.broadcasted_iota(jnp.int32, shape, 1)


def row_iota(shape):
    return lax.broadcasted_iota(jnp.int32, shape, 0)


def pack_kernel(tiles, asked, win, width, me_ref, owner_ref, *refs):
    offs = refs[:asked]
    obj_ref = refs[asked]
    outs = refs[asked + 1 : 2 * asked + 1]
    buf, pack, params, in_sem, out_sem = refs[2 * asked + 1 :]
    half = win // 2
    quarter = win // 4
    strip = strip_held(owner_ref, me_ref[0], tiles)

    def fetch(k):
        start = pl.multiple_of(params[k, 3], 128)
        return pltpu.make_async_copy(
            obj_ref.at[:, :, pl.ds(start, 2 * win)], buf.at[k], in_sem.at[k]
        )

    for k in range(asked):
        y_up, x_up, x_low, _ = geometry(offs[k][0, 0], offs[k][0, 1], offs[k][1, 0], offs[k][1, 1])
        left = jnp.minimum(x_up, x_low)
        params[k, 0] = y_up
        params[k, 1] = (x_low > x_up).astype(jnp.int32)
        params[k, 3] = jnp.minimum((left // 128) * 128, width - 2 * win)
        params[k, 2] = left - params[k, 3]
        fetch(k).start()

    def one(k, carry):
        fetch(k).wait()
        y_up = params[k, 0]
        right = params[k, 1]
        rem = params[k, 2]
        turn = lax.rem(half - rem, half)
        keep = lane_iota((quarter, half)) < half - rem
        base = strip * win
        for part in range(2):
            for chunk in range(2):
                outer = []
                for level in range(2):
                    row0 = level * half + chunk * quarter
                    wide = buf[k, part, row0 : row0 + quarter, :].astype(jnp.float32)
                    spun = [
                        pltpu.roll(wide[:, half * b : half * (b + 1)], turn, 1) for b in range(4)
                    ]
                    cols = [jnp.where(keep, spun[b], spun[b + 1]) for b in range(3)]
                    rows = base + row0 + row_iota((quarter, half))
                    in_upper = (rows < y_up + win).astype(jnp.int32)
                    low_first = in_upper == right
                    pack[k, part, row0 : row0 + quarter, 0:half] = jnp.where(
                        low_first, cols[0], cols[1]
                    ).astype(pack.dtype)
                    pack[k, part, row0 : row0 + quarter, half:win] = jnp.where(
                        low_first, cols[1], cols[2]
                    ).astype(pack.dtype)
                    outer.append(jnp.where(right == 1, cols[2], cols[0]))
                high = base + half + chunk * quarter + row_iota((quarter, half))
                use_high = (high >= y_up + half) & (high < y_up + win)
                pack[k, part, win : win + quarter, half * chunk : half * (chunk + 1)] = jnp.where(
                    use_high, outer[1], outer[0]
                ).astype(pack.dtype)
        return carry

    for k in range(asked):
        one(k, 0)
        pltpu.make_async_copy(pack.at[k], outs[k], out_sem.at[k]).start()
    for k in range(asked):
        pltpu.make_async_copy(pack.at[k], outs[k], out_sem.at[k]).wait()


def halves(x):
    high = x.astype(jnp.bfloat16)
    return high, (x - high.astype(jnp.float32)).astype(jnp.bfloat16)


def dot(a, b):
    return lax.dot_general(a, b, (((1,), (0,)), ((), ())), preferred_element_type=jnp.float32)


def rows_from(ref, part, start, count):
    down = pl.multiple_of((start // 8) * 8, 8)
    rows = ref[part, pl.ds(down, count + 8), :]
    return pltpu.roll(rows, lax.rem(count + 8 - (start - down), count + 8), 0)[0:count]


def rows_to(ref, part, start, blocks):
    down = pl.multiple_of((start // 8) * 8, 8)
    rows = jnp.concatenate(blocks + [jnp.zeros((8, blocks[0].shape[1]), jnp.float32)], axis=0)
    ref[part, pl.ds(down, rows.shape[0]), :] = pltpu.roll(rows, start - down, 0)


LEVELS = 32600.0
CODE_UNIT = 256.0


def code_of(peak):
    return jnp.ceil(jnp.log(jnp.maximum(peak, 1e-30)) * (CODE_UNIT / math.log(2.0)))


def step_of(code):
    return jnp.exp(code * (math.log(2.0) / CODE_UNIT)) * (1.0 / LEVELS)


def column_peak(x):
    return jnp.max(jnp.abs(x), axis=0, keepdims=True)


def to_levels(x, code):
    return jnp.floor(x * (1.0 / step_of(code)) + 0.5).astype(jnp.int32).astype(jnp.int16)


def code_rows(codes):
    rest = jnp.zeros((16 - len(codes), codes[0].shape[1]), jnp.float32)
    return jnp.concatenate(codes + [rest], axis=0).astype(jnp.int32).astype(jnp.int16)


def wide_of(x):
    return x.astype(jnp.int32).astype(jnp.float32)


def compute_kernel(tiles, pos_groups, win, modes, grad_scale, me_ref, owner_ref, off_ref, *refs):
    packs = refs[:tiles]
    probe, amp, prop_re, prop_im, prop_t_re, prop_t_im, spot_ref = refs[tiles : tiles + 7]
    grads = refs[tiles + 7 : 2 * tiles + 7]
    away_ref, kept_ref = refs[2 * tiles + 7 : 2 * tiles + 9]
    (
        held, cat, wins, far, factor, right_m, left_m, obj_acc, probe_acc, gcat, outer_acc, gpack,
        in_sem, out_sem, piece_sem,
    ) = refs[2 * tiles + 9 :]
    half = win // 2
    quarter = win // 4
    me = me_ref[0]
    fetches = [pltpu.make_async_copy(packs[k], held.at[k], in_sem.at[k]) for k in range(tiles)]
    for fetch in fetches:
        fetch.start()

    for way in range(2):
        if way == 0:
            right, left = (prop_t_re[...], prop_t_im[...]), (prop_re[...], prop_im[...])
        else:
            right, left = (prop_re[...], -prop_im[...]), (prop_t_re[...], -prop_t_im[...])
        for at, (r, l) in enumerate(zip(right + (right[0] + right[1],), left + (left[0] + left[1],))):
            r_h, r_l = halves(r)
            l_h, l_l = halves(l)
            for third, (rr, ll) in enumerate([(r_h, l_h), (r_h, l_h), (r_l, l_l)]):
                right_m[way, at, third * win : (third + 1) * win, :] = rr
                left_m[way, at, :, third * win : (third + 1) * win] = ll

    y_up, x_up, x_low, first = geometry(off_ref[0, 0], off_ref[0, 1], off_ref[1, 0], off_ref[1, 1])
    right = x_low > x_up
    strip = y_up // win
    rem = y_up - strip * win
    low_rem = lax.rem(rem, half)
    mid_block = (y_up + half) // half

    def slot_of(s):
        return lax.rem(me - owner_ref[jnp.minimum(s, tiles - 1)] + tiles, tiles)

    for fetch in fetches:
        fetch.wait()
    slots = [slot_of(strip + d) for d in range(3)]
    for part in range(2):
        for d in range(3):
            cat[part, d * win : (d + 1) * win, :] = held[slots[d], part, 0:win, :].astype(jnp.float32)
        for d in range(2):
            slot = slot_of((mid_block + d) // 2)
            for chunk in range(2):
                outer_acc[part, d * half + chunk * quarter : d * half + (chunk + 1) * quarter, :] = held[
                    slot, part, win : win + quarter, half * chunk : half * (chunk + 1)
                ].astype(jnp.float32)
    for part in range(2):
        upper = rows_from(cat, part, rem, win)
        wins[0, part] = upper
        wins[1, part, half:win, :] = rows_from(cat, part, rem + win, half)
        outer = rows_from(outer_acc, part, low_rem, half)
        wins[1, part, 0:half, 0:half] = jnp.where(right, upper[half:win, half:win], outer)
        wins[1, part, 0:half, half:win] = jnp.where(right, outer, upper[half:win, 0:half])

    def three(re, im, side):
        both_re, both_im, both_sum = side(re, 0), side(im, 1), side(re + im, 2)
        return both_re - both_im, both_sum - both_re - both_im

    def both(way, re, im):
        def from_right(x, at):
            high, low = halves(x)
            return dot(jnp.concatenate([high, low, high], axis=1), right_m[way, at])

        def from_left(x, at):
            high, low = halves(x)
            return dot(left_m[way, at], jnp.concatenate([high, low, high], axis=0))

        return three(*three(re, im, from_right), from_left)

    def forward(n, carry):
        q = n // modes
        m = lax.rem(n, modes)
        p_re, p_im = probe[m, 0], probe[m, 1]
        w_re, w_im = wins[q, 0], wins[q, 1]
        far[n, 0:win, :], far[n, win : 2 * win, :] = both(0, p_re * w_re - p_im * w_im, p_re * w_im + p_im * w_re)
        return carry

    lax.fori_loop(0, 2 * modes, forward, 0, unroll=2)
    for q in range(2):
        total = jnp.zeros((win, win), jnp.float32)
        for m in range(modes):
            f_re, f_im = far[q * modes + m, 0:win, :], far[q * modes + m, win : 2 * win, :]
            total = total + (f_re * f_re + f_im * f_im)
        frame = jnp.where(first, q, 1 - q)
        measured = amp[frame]
        factor[q] = (1.0 - measured * lax.rsqrt(jnp.maximum(total, 1.0))) * grad_scale
    obj_acc[...] = jnp.zeros_like(obj_acc)
    probe_acc[...] = jnp.zeros_like(probe_acc)

    def backward(n, carry):
        q = n // modes
        m = lax.rem(n, modes)
        scale = factor[q]
        b_re, b_im = both(1, far[n, 0:win, :] * scale, far[n, win : 2 * win, :] * scale)
        p_re, p_im = probe[m, 0], probe[m, 1]
        w_re, w_im = wins[q, 0], wins[q, 1]
        obj_acc[q, 0] = obj_acc[q, 0] + (p_re * b_re + p_im * b_im)
        obj_acc[q, 1] = obj_acc[q, 1] + (p_re * b_im - p_im * b_re)
        probe_acc[m, 0] = probe_acc[m, 0] + (w_re * b_re + w_im * b_im)
        probe_acc[m, 1] = probe_acc[m, 1] + (w_re * b_im - w_im * b_re)
        return carry

    lax.fori_loop(0, 2 * modes, backward, 0, unroll=2)
    share = win // pos_groups
    spot = spot_ref[0]
    piece_copies = []
    for j in range(pos_groups):
        start = pl.multiple_of(jnp.bitwise_xor(spot, j) * share, share)
        home = (away_ref if j % 2 else kept_ref).at[j // 2]
        piece_copies.append(
            pltpu.make_async_copy(probe_acc.at[:, :, pl.ds(start, share), :], home, piece_sem.at[j])
        )
        piece_copies[-1].start()

    gcat[...] = jnp.zeros_like(gcat)
    outer_acc[...] = jnp.zeros_like(outer_acc)
    for part in range(2):
        low_a = obj_acc[1, part, 0:half, 0:half]
        low_b = obj_acc[1, part, 0:half, half:win]
        zero = jnp.zeros_like(low_a)
        obj_acc[0, part, half:win, 0:half] += jnp.where(right, zero, low_b)
        obj_acc[0, part, half:win, half:win] += jnp.where(right, low_a, zero)
        rows_to(gcat, part, rem, [obj_acc[0, part], obj_acc[1, part, half:win, :]])
        rows_to(outer_acc, part, low_rem, [jnp.where(right, low_b, low_a)])
        outer = outer_acc[part, 0:half, :] + outer_acc[part, half:win, :]
        outer_code = code_of(column_peak(outer))
        outer_levels = to_levels(outer, outer_code)
        for d in range(3):
            codes = []
            for level in range(2):
                rows = gcat[part, d * win + level * half : d * win + (level + 1) * half, :]
                codes.append(code_of(column_peak(rows)))
                gpack[d, part, level * half : (level + 1) * half, :] = to_levels(rows, codes[-1])
            for chunk in range(2):
                gpack[d, part, win : win + quarter, half * chunk : half * (chunk + 1)] = outer_levels[
                    chunk * quarter : (chunk + 1) * quarter, :
                ]
            codes.append(jnp.concatenate([outer_code, outer_code], axis=1))
            gpack[d, part, win + quarter : win + quarter + 16, :] = code_rows(codes)
    grad_copies = []
    for k in range(tiles):
        there = strip_held(owner_ref, lax.rem(me + k, tiles), tiles)
        d = jnp.clip(there - strip, 0, 2)
        grad_copies.append(pltpu.make_async_copy(gpack.at[d], grads[k], out_sem.at[k]))
        grad_copies[-1].start()
    for copy in piece_copies + grad_copies:
        copy.wait()


def propagate_call(tiles, pos_groups, win, modes, grad_scale):
    half = win // 2
    share = win // pos_groups
    pack_shape = (2, win + win // 4, win)
    grad_shape = (2, win + win // 4 + 16, win)
    smem = pl.BlockSpec(memory_space=pltpu.SMEM)
    vmem = pl.BlockSpec(memory_space=pltpu.VMEM)
    anywhere = pl.BlockSpec(memory_space=pl.ANY)
    return pl.pallas_call(
        functools.partial(compute_kernel, tiles, pos_groups, win, modes, grad_scale),
        out_shape=[jax.ShapeDtypeStruct(grad_shape, jnp.int16)] * tiles
        + [jax.ShapeDtypeStruct((pos_groups // 2, modes, 2, share, win), jnp.float32)] * 2,
        in_specs=[smem] * 3 + [anywhere] * tiles + [vmem] * 6 + [smem],
        out_specs=[anywhere] * (tiles + 2),
        scratch_shapes=[
            pltpu.VMEM((tiles,) + pack_shape, jnp.bfloat16),
            pltpu.VMEM((2, 3 * win, win), jnp.float32),
            pltpu.VMEM((2, 2, win, win), jnp.float32),
            pltpu.VMEM((2 * modes, 2 * win, win), jnp.float32),
            pltpu.VMEM((2, win, win), jnp.float32),
            pltpu.VMEM((2, 3, 3 * win, win), jnp.bfloat16),
            pltpu.VMEM((2, 3, win, 3 * win), jnp.bfloat16),
            pltpu.VMEM((2, 2, win, win), jnp.float32),
            pltpu.VMEM((modes, 2, win, win), jnp.float32),
            pltpu.VMEM((2, 3 * win, win), jnp.float32),
            pltpu.VMEM((2, win, half), jnp.float32),
            pltpu.VMEM((3,) + grad_shape, jnp.int16),
            pltpu.SemaphoreType.DMA((tiles,)),
            pltpu.SemaphoreType.DMA((tiles,)),
            pltpu.SemaphoreType.DMA((pos_groups,)),
        ],
        compiler_params=grant(40),
        name="propagate",
    )


def packed(total, pack_ref, b, rows):
    code = code_of(column_peak(total))
    pack_ref[b * rows : (b + 1) * rows, :] = to_levels(total, code)
    return code


def probe_cross_kernel(blocks, rows, kept_ref, came_ref, total_ref, pack_ref):
    codes = []
    for b in range(blocks):
        total_ref[b] = kept_ref[0, b] + came_ref[0, b]
        codes.append(packed(kept_ref[1, b] + came_ref[1, b], pack_ref, b, rows))
    pack_ref[blocks * rows : blocks * rows + 16, :] = code_rows(codes)


def unpacked(pack_ref, scale, b, rows):
    return wide_of(pack_ref[b * rows : (b + 1) * rows, :]) * scale[b : b + 1, :]


def probe_scale(pack_ref, blocks, rows):
    return step_of(wide_of(pack_ref[blocks * rows : blocks * rows + 16, :]))


def probe_close_kernel(blocks, rows, kept_ref, came_ref, pack_ref):
    scale = probe_scale(came_ref, blocks, rows)
    codes = [
        packed(kept_ref[b] + unpacked(came_ref, scale, b, rows), pack_ref, b, rows) for b in range(blocks)
    ]
    pack_ref[blocks * rows : blocks * rows + 16, :] = code_rows(codes)


def probe_merge_kernel(blocks, rows, own_ref, came_ref, pack_ref):
    own, came = probe_scale(own_ref, blocks, rows), probe_scale(came_ref, blocks, rows)
    codes = [
        packed(unpacked(own_ref, own, b, rows) + unpacked(came_ref, came, b, rows), pack_ref, b, rows)
        for b in range(blocks)
    ]
    pack_ref[blocks * rows : blocks * rows + 16, :] = code_rows(codes)


def probe_sum_kernel(blocks, rows, own_ref, came_ref, total_ref):
    own, came = probe_scale(own_ref, blocks, rows), probe_scale(came_ref, blocks, rows)
    for b in range(blocks):
        total_ref[b] = unpacked(own_ref, own, b, rows) + unpacked(came_ref, came, b, rows)


def place_kernel(tiles, spots, steps_back, first, win, slab, me_ref, spot_ref, owner_ref, *refs):
    picks = [(j, k) for k in steps_back for j in range(spots)]
    count = len(picks)
    offs, refs = refs[:spots], refs[spots:]
    packs, refs = refs[:count], refs[count:]
    if not first:
        before, refs = refs[0], refs[1:]
    out_ref, held, acc, params, in_sem, out_sem = refs
    half = win // 2
    quarter = win // 4
    me = me_ref[0]
    strip = strip_held(owner_ref, me, tiles)
    base = strip * win
    first_col = spot_ref[0] * slab
    margin = 2 * win
    span = 3 * half
    if not first:
        resume = pltpu.make_async_copy(before, acc.at[:, :, margin : margin + slab], out_sem)
        resume.start()
    for n, (j, k) in enumerate(picks):
        off = offs[j]
        y_up, x_up, x_low, _ = geometry(off[2 * k, 0], off[2 * k, 1], off[2 * k + 1, 0], off[2 * k + 1, 1])
        left = jnp.minimum(x_up, x_low)
        hit = (y_up < base + win) & (y_up + span > base) & (left < first_col + slab) & (left + span > first_col)
        params[n, 0] = hit.astype(jnp.int32)
        params[n, 1] = y_up
        params[n, 2] = (x_low > x_up).astype(jnp.int32)
        params[n, 3] = left - first_col + margin

        @pl.when(hit)
        def _():
            pltpu.make_async_copy(packs[n], held.at[n], in_sem.at[n]).start()

    def clear(i, carry):
        acc[:, pl.ds(pl.multiple_of(i * 8, 8), 8), :] = jnp.zeros((2, 8, acc.shape[2]), jnp.float32)
        return carry

    if first:
        lax.fori_loop(0, win // 8, clear, 0)
    else:
        resume.wait()

    def one(n, carry):
        @pl.when(params[n, 0] == 1)
        def _():
            pltpu.make_async_copy(packs[0], held.at[n], in_sem.at[n]).wait()
            y_up = params[n, 1]
            right = params[n, 2]
            col = params[n, 3]
            start = pl.multiple_of((col // 128) * 128, 128)
            rem = col - start
            lanes = lane_iota((quarter, half))
            stay = lanes >= rem

            def strip_piece(part, chunk, steps):
                row0 = chunk * quarter
                level = chunk // 2
                rows = base + row0 + row_iota((quarter, half))
                low_first = (rows < y_up + win).astype(jnp.int32) == right
                in_outer = (rows >= y_up + half) & (rows < y_up + win)
                main = wide_of(held[n, part, row0 : row0 + quarter, :]) * steps[level : level + 1, :]
                m0 = main[:, 0:half]
                m1 = main[:, half:win]
                side = held[n, part, win : win + quarter, half * (chunk % 2) : half * (chunk % 2 + 1)]
                side = jnp.where(in_outer, wide_of(side) * steps[2:3, 0:half], 0.0)
                cols = [
                    jnp.where(low_first, m0, jnp.where(right == 0, side, 0.0)),
                    jnp.where(low_first, m1, m0),
                    jnp.where(low_first, jnp.where(right == 1, side, 0.0), m1),
                ]
                spun = [pltpu.roll(c, rem, 1) for c in cols]
                zero = jnp.zeros_like(m0)
                moved = [
                    jnp.where(stay, spun[0], zero),
                    jnp.where(stay, spun[1], spun[0]),
                    jnp.where(stay, spun[2], spun[1]),
                    jnp.where(stay, zero, spun[2]),
                ]
                for b in range(4):
                    at = pl.ds(pl.multiple_of(start + b * half, 128), half)
                    acc[part, row0 : row0 + quarter, at] += moved[b]

            steps = [step_of(wide_of(held[n, part, win + quarter : win + quarter + 16, :])) for part in range(2)]
            for chunk in range(4):
                low = base + chunk * quarter

                @pl.when((low < y_up + span) & (low + quarter > y_up))
                def _():
                    for part in range(2):
                        strip_piece(part, chunk, steps[part])

        return carry

    lax.fori_loop(0, count, one, 0)
    out = pltpu.make_async_copy(acc.at[:, :, margin : margin + slab], out_ref, out_sem)
    out.start()
    out.wait()


def shifted(x, axis, count, k):
    return lax.ppermute(x, axis, [(i, (i + k) % count) for i in range(count)])


def swapped(x, axis, count, bit):
    return lax.ppermute(x, axis, [(i, i ^ bit) for i in range(count)])


def per_device_packed(object_field, probe, amplitude, offsets, strip_owner, chirp):
    tiles = lax.axis_size("tile")
    pos_groups = lax.axis_size("pos")
    pos_count, win, _ = amplitude.shape
    modes = probe.shape[0]
    width = object_field.shape[2]
    slab = width // pos_groups
    quarter = win // 4
    grad_scale = 1.0 / math.sqrt(pos_count * tiles * pos_groups)
    me = lax.axis_index("tile").astype(jnp.int32).reshape(1)
    spot = lax.axis_index("pos").astype(jnp.int32).reshape(1)
    smem = pl.BlockSpec(memory_space=pltpu.SMEM)
    vmem = pl.BlockSpec(memory_space=pltpu.VMEM)
    anywhere = pl.BlockSpec(memory_space=pl.ANY)
    pack_shape = (2, win + quarter, win)
    grad_shape = (2, win + quarter + 16, win)
    share = win // pos_groups

    offs = [offsets] + [shifted(offsets, "tile", tiles, tiles - k) for k in range(1, tiles)]

    def pack_for(asking, field):
        asked = len(asking)
        return pl.pallas_call(
            functools.partial(pack_kernel, tiles, asked, win, width),
            out_shape=[jax.ShapeDtypeStruct(pack_shape, jnp.bfloat16)] * asked,
            in_specs=[smem] * (2 + asked) + [pl.BlockSpec(memory_space=pltpu.HBM)],
            out_specs=[anywhere] * asked,
            scratch_shapes=[
                pltpu.VMEM((asked, 2, win, 2 * win), jnp.bfloat16),
                pltpu.VMEM((asked,) + pack_shape, jnp.bfloat16),
                pltpu.SMEM((asked, 4), jnp.int32),
                pltpu.SemaphoreType.DMA((asked,)),
                pltpu.SemaphoreType.DMA((asked,)),
            ],
            compiler_params=grant(8),
            name="pack",
        )(me, strip_owner, *asking, pltpu.with_memory_space_constraint(field, pltpu.HBM))

    near_first = near_to_far(tiles)
    packs = [None] * tiles
    for k in near_first:
        packs[k] = pack_for(offs[k : k + 1], object_field)[0]
    own_off, chirp, _ = lax.optimization_barrier((offsets, chirp, packs[near_first[-1]]))
    packs[0] = pack_for([own_off], object_field)[0]
    column_offs = [jnp.concatenate([own_off] + [offs[tiles - k] for k in range(1, tiles)], axis=0)]
    bit = pos_groups // 2
    while bit:
        column_offs = column_offs + [swapped(o, "pos", pos_groups, bit) for o in column_offs]
        bit //= 2
    arrived = [packs[0]] + [shifted(packs[k], "tile", tiles, k) for k in range(1, tiles)]
    prop_re, prop_im = build_propagator(chirp)
    measured = lax.optimization_barrier((amplitude, chirp))[0].astype(jnp.float32)
    arrived, column_offs = lax.optimization_barrier((arrived, column_offs))
    results = propagate_call(tiles, pos_groups, win, modes, grad_scale)(
        me, strip_owner, offsets, *arrived, probe, measured, prop_re, prop_im, prop_re.T, prop_im.T, spot
    )
    grads, (away, kept) = results[:tiles], results[tiles:]

    column = [grads[0]] + [shifted(grads[k], "tile", tiles, k) for k in range(1, tiles)]
    columns = [column]
    bit = pos_groups // 2
    while bit:
        columns = columns + [[swapped(x, "pos", pos_groups, bit) for x in column] for column in columns]
        bit //= 2

    blocks = modes * 2

    whole = jax.ShapeDtypeStruct((blocks, share, win), jnp.float32)
    coded = jax.ShapeDtypeStruct((blocks * share + 16, win), jnp.int16)

    def probe_step(kernel, out_shape, *parts):
        return pl.pallas_call(
            functools.partial(kernel, blocks, share), out_shape=out_shape, compiler_params=grant(8)
        )(*parts)

    pair = (2, blocks, share, win)
    came = swapped(away, "pos", pos_groups, 1).reshape(pair)
    probe_own, probe_pack = probe_step(probe_cross_kernel, [whole, coded], kept.reshape(pair), came)
    came = swapped(probe_pack, "pos", pos_groups, 2)
    probe_pack = probe_step(probe_close_kernel, coded, probe_own, came)
    bit = 1
    while 2 * bit < tiles:
        came = swapped(probe_pack, "tile", tiles, bit)
        probe_pack = probe_step(probe_merge_kernel, coded, probe_pack, came)
        bit *= 2
    came = swapped(probe_pack, "tile", tiles, bit)
    probe_out = probe_step(probe_sum_kernel, whole, probe_pack, came)

    spots = len(columns)
    placed = None
    near_first = near_to_far(tiles)
    for steps_back in ([0], near_first[:-1], near_first[-1:]):
        arrays = [columns[j][k] for k in steps_back for j in range(spots)]
        count = len(arrays)
        first = placed is None
        placed = pl.pallas_call(
            functools.partial(place_kernel, tiles, spots, steps_back, first, win, slab),
            out_shape=jax.ShapeDtypeStruct((2, win, slab), jnp.float32),
            in_specs=[smem] * (3 + spots) + [anywhere] * (count + (not first)),
            out_specs=anywhere,
            scratch_shapes=[
                pltpu.VMEM((count,) + grad_shape, jnp.int16),
                pltpu.VMEM((2, win, slab + 4 * win), jnp.float32),
                pltpu.SMEM((count, 4), jnp.int32),
                pltpu.SemaphoreType.DMA((count,)),
                pltpu.SemaphoreType.DMA,
            ],
            compiler_params=grant(16),
        )(me, spot, strip_owner, *column_offs, *arrays, *([] if first else [placed]))
    return (placed, probe_out.reshape(modes, 2, share, win))


def per_device(object_field, probe, amplitude, offsets, strip_owner, chirp):
    tiles = lax.axis_size("tile")
    pos_groups = lax.axis_size("pos")
    pos_count, win, _ = amplitude.shape
    width = object_field.shape[2]
    packed = (
        pos_count == 2
        and object_field.shape[1] == win
        and win == 256
        and width // pos_groups >= 2 * win
        and (width // pos_groups) % 128 == 0
        and pos_groups == 4
        and tiles & (tiles - 1) == 0
        and tiles >= 4
        and (win // pos_groups) % 16 == 0
    )
    if not packed:
        return per_device_general(object_field, probe, amplitude, offsets, strip_owner, chirp)
    return per_device_packed(object_field, probe, amplitude, offsets, strip_owner, chirp)


def near_to_far(tiles):
    return sorted(range(1, tiles), key=lambda k: (min(k, tiles - k), k))


def solution(mesh):
    return jax.shard_map(
        per_device,
        mesh=mesh,
        in_specs=(
            P(None, ("groups", "tile"), None),
            P("groups", None, None, None),
            P(("groups", "tile", "pos"), None, None),
            P(("groups", "tile", "pos"), None),
            P("groups"),
            P(),
        ),
        out_specs=(P(None, ("groups", "tile"), "pos"), P("groups", None, "pos", None)),
        check_vma=False,
    )
```
